1024 devices in a mesh: space: 64 (over x, z_hi, y, core), chan: 16 (over z_lo).
Axes of the slice: x: 4, y: 4, z: 32 (z_hi: 2, z_lo: 16; z = z_hi * 16 + z_lo), core: 2. Of those that a mesh axis runs over, the one named last changes fastest.
Arguments:
- volume: bfloat16 [32, 128, 32, 128], P(None, 'space', 'chan'), may hold values from -6 to 6
- weight_first: bfloat16 [3, 3, 3, 64, 32], replicated, may hold values from -0.21875 to 0.21875
- weight_deep: bfloat16 [3, 3, 3, 512, 64], P(None, None, None, 'chan'), may hold values from -0.15625 to 0.15625
- cotangent: bfloat16 [512, 64, 1024], P('chan', 'space'), may hold values from -6 to 6
Outputs:
- deep_out: bfloat16 [512, 64, 1024], P('chan', 'space')
- grad_deep: float32 [3, 3, 3, 512, 64], P(None, None, None, 'chan')
The draws below stay inside these ranges and needn't reach their ends.
All inputs are finite; a program needn't handle non-finite values.
Results may differ from the reference program's by a relative error of at most 0.0051.
Values may be sent and summed in bfloat16 or wider, within the bound.
A program may use at most 32 MiB of HBM per device.

```python
import jax
import jax.numpy as jnp
from jax import lax

CIN = 32
CMID = 64
COUT = 512
NZ = 128
NX = 128
NY = 32
MX = 64
MY = 16
MZ = 64


def steps_of(stream_key, dims, split, least, high):
    def one(axis_at, parts):
        draws = jax.random.uniform(jax.random.fold_in(jax.random.fold_in(stream_key, 6), axis_at), (parts,), jnp.float32, least / len(split), high / len(split))
        return jnp.repeat(jnp.exp(draws), dims[axis_at] // parts).reshape((-1,) + (1,) * (len(dims) - axis_at - 1))

    level = one(*split[0])
    for cut in split[1:]:
        level = level * one(*cut)
    return level


def gaussian(stream_key, shape, spread, bound, shards=(), kind=jnp.bfloat16):
    loudness = steps_of(stream_key, shape, shards, -0.22, 0.18) if shards else 1.0
    entries = jax.random.normal(stream_key, shape, jnp.float32) * spread * loudness
    return jnp.minimum(jnp.maximum(entries, -bound), bound).astype(kind)


def setup_inputs(seed: int = 0) -> dict:
    keys = jax.random.split(jax.random.key(seed), 5)
    return {
        "volume": gaussian(keys[0], (CIN, NX, NY, NZ), 1.0, 6.0, ((1, 64), (2, 16))),
        "weight_first": gaussian(keys[1], (3, 3, 3, CMID, CIN), (27 * CIN) ** -0.5, 0.21875),
        "weight_deep": gaussian(keys[2], (3, 3, 3, COUT, CMID), (27 * CMID) ** -0.5, 0.15625, ((3, 16),)),
        "cotangent": gaussian(keys[3], (COUT, MX, MY * MZ), 1.0, 6.0, ((0, 16), (1, 64))),
    }


def convolve(padded, weight, planes, rows, depth):
    total = jnp.zeros((weight.shape[3], planes, rows, depth), jnp.float32)
    for offset_x in range(3):
        for offset_y in range(3):
            for offset_z in range(3):
                window = padded[:, offset_x:offset_x + planes, offset_y:offset_y + rows, offset_z:offset_z + depth]
                total = total + jnp.einsum("oc,cxyz->oxyz", weight[offset_x, offset_y, offset_z].astype(jnp.float32), window.astype(jnp.float32))
    return total


def weight_terms(grad_pre, padded, planes, rows, depth):
    outer = []
    for offset_x in range(3):
        middle = []
        for offset_y in range(3):
            inner = []
            for offset_z in range(3):
                window = padded[:, offset_x:offset_x + planes, offset_y:offset_y + rows, offset_z:offset_z + depth]
                inner.append(jnp.einsum("oxyz,cxyz->oc", grad_pre.astype(jnp.float32), window.astype(jnp.float32)))
            middle.append(jnp.stack(inner))
        outer.append(jnp.stack(middle))
    return jnp.stack(outer)


def pool_mean(act):
    chans, planes, rows, depth = act.shape
    blocks = act.reshape(chans, planes // 2, 2, rows // 2, 2, depth // 2, 2)
    return jnp.mean(blocks, axis=(2, 4, 6))


def reference(volume, weight_first, weight_deep, cotangent):
    padded_in = jnp.pad(volume, ((0, 0), (1, 1), (1, 1), (1, 1)))

    def first_block(index):
        slab = lax.dynamic_slice_in_dim(padded_in, (index * 2).astype(jnp.int32), 4, axis=1)
        pre_first = convolve(slab, weight_first, 2, NY, NZ)
        return pool_mean(jax.nn.silu(pre_first)).astype(jnp.bfloat16)

    blocks = lax.map(first_block, jnp.arange(MX, dtype=jnp.int32))
    pooled = jnp.moveaxis(blocks[:, :, 0], 0, 1)
    padded_pool = jnp.pad(pooled, ((0, 0), (1, 1), (1, 1), (1, 1)))

    def deep_plane(grad, index):
        slab = lax.dynamic_slice_in_dim(padded_pool, index.astype(jnp.int32), 3, axis=1)
        pre_deep = convolve(slab, weight_deep, 1, MY, MZ)
        out = jax.nn.silu(pre_deep).astype(jnp.bfloat16)
        cot_flat = lax.dynamic_slice_in_dim(cotangent, index.astype(jnp.int32), 1, axis=1)
        cot = cot_flat.reshape(COUT, 1, MY, MZ).astype(jnp.float32)
        sigma = jax.nn.sigmoid(pre_deep)
        grad_pre = (cot * sigma * (1.0 + pre_deep * (1.0 - sigma))).astype(jnp.bfloat16)
        grad = grad + weight_terms(grad_pre, slab, 1, MY, MZ)
        return grad, out

    start = jnp.zeros((3, 3, 3, COUT, CMID), jnp.float32)
    grad_deep, outs = lax.scan(deep_plane, start, jnp.arange(MX, dtype=jnp.int32))
    deep_out = jnp.moveaxis(outs[:, :, 0], 0, 1).reshape(COUT, MX, MY * MZ)
    return deep_out, grad_deep
```

```python
import jax
import jax.numpy as jnp
from jax import lax
from jax.experimental import pallas as pl
from jax.experimental.pallas import tpu as pltpu
from jax.sharding import PartitionSpec as P


def padded_2(array, sides, width):
    for axis, dim in sides:
        peers, length = (lax.axis_size(axis), array.shape[dim])
        up = [(i, (i + 1) % peers) for i in range(peers - 1)]
        down = [(j, i) for i, j in up]
        last = lax.slice_in_dim(array, length - width, length, axis=dim)
        leading = lax.slice_in_dim(array, 0, width, axis=dim)
        before = lax.ppermute(last, axis, up)
        after = lax.ppermute(leading, axis, down)
        array = jnp.concatenate([before, array, after], axis=dim)
    return array


def convolve(padded, weight, planes, rows, depth):
    total = jnp.zeros((weight.shape[3], planes, rows, depth), jnp.float32)
    for offset_x in range(3):
        for offset_y in range(3):
            for offset_z in range(3):
                window = padded[
                    :,
                    offset_x : offset_x + planes,
                    offset_y : offset_y + rows,
                    offset_z : offset_z + depth,
                ]
                total = total + jnp.einsum(
                    "oc,cxyz->oxyz",
                    weight[offset_x, offset_y, offset_z],
                    window,
                    preferred_element_type=jnp.float32,
                )
    return total


def weight_terms(grad_pre, padded, planes, rows, depth):
    outer = []
    for offset_x in range(3):
        middle = []
        for offset_y in range(3):
            inner = []
            for offset_z in range(3):
                window = padded[
                    :,
                    offset_x : offset_x + planes,
                    offset_y : offset_y + rows,
                    offset_z : offset_z + depth,
                ]
                inner.append(
                    jnp.einsum(
                        "oxyz,cxyz->oc", grad_pre, window, preferred_element_type=jnp.float32
                    )
                )
            middle.append(jnp.stack(inner))
        outer.append(jnp.stack(middle))
    return jnp.stack(outer)


def pool_mean(act):
    chans, planes, rows, depth = act.shape
    blocks = act.reshape(chans, planes // 2, 2, rows // 2, 2, depth // 2, 2)
    return jnp.mean(blocks, axis=(2, 4, 6))


MESH = pl.DeviceIdType.MESH
CHUNKS = 27
PLANE = 32


def place(index, high):
    return (index // 8) * 16 + high * 8 + index % 8


def reduce_kernel(terms, total, parts, mine, far, sums, sems):
    space = lax.axis_index("space")
    high = (space // 8) % 2
    here = (space // 16) * 8 + space % 8
    other = place(here, 1 - high)
    barrier = pltpu.get_barrier_semaphore()

    def peer(step):
        return (here + step) % PLANE

    for step in range(1, PLANE):
        pl.semaphore_signal(
            barrier, inc=1, device_id={"space": place(peer(step), high)}, device_id_type=MESH
        )
    pl.semaphore_signal(barrier, inc=1, device_id={"space": other}, device_id_type=MESH)
    pl.semaphore_wait(barrier, PLANE)
    owner = here < CHUNKS

    for step in range(1, PLANE):
        to = peer(step)

        @pl.when(to < CHUNKS)
        def _():
            pltpu.make_async_remote_copy(
                terms.at[to],
                parts.at[here],
                sems.at[0],
                sems.at[1],
                device_id={"space": place(to, high)},
                device_id_type=MESH,
            ).start()

    def sized(ref, sem):
        return pltpu.make_async_copy(ref, ref, sem)

    @pl.when(owner)
    def _():
        parts[here] = terms[here]
        sized(parts.at[pl.ds(0, PLANE - 1)], sems.at[1]).wait()
        mine[...] = jnp.sum(parts[...], axis=0)
        swap = pltpu.make_async_remote_copy(
            mine, far, sems.at[2], sems.at[3], device_id={"space": other}, device_id_type=MESH
        )
        swap.start()
        swap.wait()
        sums[here] = mine[...] + far[...]
        for step in range(1, PLANE):
            pltpu.make_async_remote_copy(
                sums.at[here],
                sums.at[here],
                sems.at[4],
                sems.at[5],
                device_id={"space": place(peer(step), high)},
                device_id_type=MESH,
            ).start()
        sized(sums.at[pl.ds(0, CHUNKS - 1)], sems.at[5]).wait()
        sized(parts.at[pl.ds(0, PLANE - 1)], sems.at[4]).wait()
        sized(terms.at[pl.ds(0, CHUNKS - 1)], sems.at[0]).wait()

    @pl.when(jnp.logical_not(owner))
    def _():
        sized(sums, sems.at[5]).wait()
        sized(terms, sems.at[0]).wait()

    total[...] = sums[...]


def reduce_space(local):
    flat = local.reshape(CHUNKS, 16, 128)
    summed = pl.pallas_call(
        reduce_kernel,
        out_shape=jax.ShapeDtypeStruct(flat.shape, jnp.float32),
        in_specs=[pl.BlockSpec(memory_space=pltpu.VMEM)],
        out_specs=pl.BlockSpec(memory_space=pltpu.VMEM),
        scratch_shapes=[
            pltpu.VMEM((PLANE, 16, 128), jnp.float32),
            pltpu.VMEM((16, 128), jnp.float32),
            pltpu.VMEM((16, 128), jnp.float32),
            pltpu.VMEM((CHUNKS, 16, 128), jnp.float32),
            pltpu.SemaphoreType.DMA((6,)),
        ],
        compiler_params=pltpu.CompilerParams(collective_id=0, has_side_effects=True),
        name="reduce_space",
    )(flat)
    return summed.reshape(local.shape)


def on_device(volume, weight_first, weight_deep, cotangent):
    planes = volume.shape[1]
    rows = volume.shape[2]
    depth = volume.shape[3]
    rimmed = padded_2(volume, (("space", 1), ("chan", 2)), 1)
    padded = jnp.pad(rimmed, ((0, 0), (0, 0), (0, 0), (1, 1)))
    pre_first = convolve(padded, weight_first, planes, rows, depth)
    pooled = pool_mean(jax.nn.silu(pre_first)).astype(jnp.bfloat16)
    whole = lax.all_gather(pooled, "chan", axis=2, tiled=True)
    framed = padded_2(whole, (("space", 1),), 1)
    deep_in = jnp.pad(framed, ((0, 0), (0, 0), (1, 1), (1, 1)))
    deep_planes = pooled.shape[1]
    deep_rows = framed.shape[2]
    deep_depth = framed.shape[3]
    pre_deep = convolve(deep_in, weight_deep, deep_planes, deep_rows, deep_depth)
    out_chans = pre_deep.shape[0]
    deep_out = (
        jax.nn.silu(pre_deep)
        .astype(jnp.bfloat16)
        .reshape(out_chans, deep_planes, deep_rows * deep_depth)
    )
    sigma = jax.nn.sigmoid(pre_deep)
    cot_grid = cotangent.reshape(out_chans, deep_planes, deep_rows, deep_depth).astype(jnp.float32)
    grad_pre = (cot_grid * sigma * (1.0 + pre_deep * (1.0 - sigma))).astype(jnp.bfloat16)
    local_grad = weight_terms(grad_pre, deep_in, deep_planes, deep_rows, deep_depth)
    grad_deep = reduce_space(local_grad)
    return (deep_out, grad_deep)


def solution(mesh):
    return jax.shard_map(
        on_device,
        mesh=mesh,
        in_specs=(
            P(None, "space", "chan", None),
            P(),
            P(None, None, None, "chan", None),
            P("chan", "space", None),
        ),
        out_specs=(P("chan", "space", None), P(None, None, None, "chan", None)),
        check_vma=False,
    )
```

```python
import jax
import jax.numpy as jnp
from jax import lax
from jax.experimental import pallas as pl
from jax.experimental.pallas import tpu as pltpu
from jax.sharding import PartitionSpec as P

MESH = pl.DeviceIdType.MESH
CHUNKS = 27
PLANE = 32
SPACE = 64
CHAN = 16
CELLS = 1024
SIDES = [(dx, dy) for dx in (-1, 0, 1) for dy in (-1, 0, 1) if (dx, dy) != (0, 0)]
SOURCE = {-1: 1, 0: pl.ds(1, 2), 1: 2}
TARGET = {-1: 3, 0: pl.ds(1, 2), 1: 0}


def place(index, high):
    return (index // 8) * 16 + high * 8 + index % 8


def at(space, chan):
    return {"space": space, "chan": chan}


def sized(ref, sem):
    return pltpu.make_async_copy(ref, ref, sem)


def dot(left, right):
    return jnp.dot(left, right, preferred_element_type=jnp.float32)


def step_kernel(
    vol_in, first_in, deep_in, cot_in, out_ref, grad_ref,
    slab, first, deep, cot, first_mat, deep_mat, windows,
    pooled, grid, products, shifted, terms, parts, mine, far, sums,
    local_sems, halo_send, halo_recv, sems,
):
    space = lax.axis_index("space")
    chan = lax.axis_index("chan")
    core = space % 2
    high = (space // 8) % 2
    here = (space // 16) * 8 + space % 8
    other = place(here, 1 - high)
    rest = chan % 4
    group = chan // 4
    side = space - 1 + 2 * core
    has_side = (side >= 0) & (side < SPACE)
    near, away = 2 * core, 2 - 2 * core

    def peer(step):
        return (here + step) % PLANE

    def exists(dx, dy):
        x, y = space + dx, chan + dy
        return (x >= 0) & (x < SPACE) & (y >= 0) & (y < CHAN)

    barrier = pltpu.get_barrier_semaphore()

    def hello(device):
        pl.semaphore_signal(barrier, inc=1, device_id=device, device_id_type=MESH)

    hello(at(other, chan))
    expected = PLANE + 9 + jnp.where(has_side, 3, 0)
    for dx, dy in SIDES:
        here_too = exists(dx, dy)
        expected = expected + jnp.where(here_too, 1, 0)

        @pl.when(here_too)
        def _():
            hello(at(space + dx, chan + dy))

    for step in range(1, 4):
        across = (group + step) % 4 * 4 + rest
        beside = group * 4 + (rest + step) % 4
        hello(at(space, across))
        hello(at(space, beside))
        hello(at(space + 1 - 2 * core, beside))

        @pl.when(has_side)
        def _():
            hello(at(side, across))

    for step in range(1, PLANE):
        hello(at(place(peer(step), high), chan))

    loads = [
        pltpu.make_async_copy(src, dst, local_sems.at[i])
        for i, (src, dst) in enumerate(
            [
                (vol_in, slab.at[pl.ds(1, 2), pl.ds(1, 2)]),
                (first_in, first),
                (deep_in, deep),
                (cot_in, cot),
            ]
        )
    ]
    for load in loads:
        load.start()

    @pl.when(space == 0)
    def _():
        slab[0] = jnp.zeros_like(slab[0])
        pooled[0] = jnp.zeros_like(pooled[0])

    @pl.when(space == SPACE - 1)
    def _():
        slab[3] = jnp.zeros_like(slab[3])
        pooled[2] = jnp.zeros_like(pooled[2])

    @pl.when(chan == 0)
    def _():
        slab[:, 0] = jnp.zeros_like(slab[:, 0])

    @pl.when(chan == CHAN - 1)
    def _():
        slab[:, 3] = jnp.zeros_like(slab[:, 3])

    for load in loads:
        load.wait()
    for a in range(3):
        for b in range(3):
            for c in range(3):
                first_mat[pl.ds((a * 3 + b) * 32, 32), pl.ds(c * 64, 64)] = first[a, b, c]
                deep_mat[pl.ds((b * 3 + c) * 32, 32), pl.ds(a * 64, 64)] = deep[a, b, c]

    pl.semaphore_wait(barrier, expected)

    def rim(n):
        dx, dy = SIDES[n]
        return pltpu.make_async_remote_copy(
            slab.at[SOURCE[dx], SOURCE[dy]],
            slab.at[TARGET[dx], TARGET[dy]],
            halo_send.at[n],
            halo_recv.at[n],
            device_id=at(space + dx, chan + dy),
            device_id_type=MESH,
        )

    for n, (dx, dy) in enumerate(SIDES):

        @pl.when(exists(dx, dy))
        def _():
            rim(n).start()

    for n, (dx, dy) in enumerate(SIDES):

        @pl.when(exists(-dx, -dy))
        def _():
            ref = slab.at[TARGET[dx], TARGET[dy]]
            sized(ref, halo_recv.at[n]).wait()

    for n, (dx, dy) in enumerate(SIDES):

        @pl.when(exists(dx, dy))
        def _():
            ref = slab.at[SOURCE[dx], SOURCE[dy]]
            sized(ref, halo_send.at[n]).wait()

    for x in range(2):
        for y in range(2):
            for a in range(3):
                for b in range(3):
                    windows[pl.ds((a * 3 + b) * 32, 32), pl.ds((x * 2 + y) * 128, 128)] = slab[
                        x + a, y + b
                    ]
    taps = lax.dot_general(
        first_mat[...], windows[...], (((0,), (0,)), ((), ())), preferred_element_type=jnp.float32
    )
    z = lax.broadcasted_iota(jnp.int32, (64, 512), 1) % 128
    pre = taps[64:128]
    pre = pre + jnp.where(z == 0, 0.0, pltpu.roll(taps[0:64], 1, 1))
    pre = pre + jnp.where(z == 127, 0.0, pltpu.roll(taps[128:192], 511, 1))
    act = pre / (1.0 + jnp.exp(-pre))
    added = act[:, 0:128] + act[:, 128:256] + act[:, 256:384] + act[:, 384:512]
    mean = ((added + pltpu.roll(added, 127, 1)) * 0.125).astype(jnp.bfloat16)
    lane = lax.broadcasted_iota(jnp.int32, (128, 128), 0)
    cell = lax.broadcasted_iota(jnp.int32, (128, 128), 1)
    left = jnp.where(lane == 2 * cell, 1.0, 0.0).astype(jnp.bfloat16)
    right = jnp.where(lane == 2 * cell - 128, 1.0, 0.0).astype(jnp.bfloat16)
    piece = dot(mean[0:32], left) + dot(mean[32:64], right)
    pooled[1, rest, group] = piece.astype(jnp.bfloat16)

    def give(src, dst, send, recv, device):
        pltpu.make_async_remote_copy(
            src, dst, sems.at[send], sems.at[recv], device_id=device, device_id_type=MESH
        ).start()

    own = pooled.at[1, rest, group]

    @pl.when(has_side)
    def _():
        for step in range(4):
            across = (group + step) % 4 * 4 + rest
            give(own, pooled.at[away, rest, group], 0, 2, at(side, across))

    for step in range(1, 4):
        across = (group + step) % 4 * 4 + rest
        give(own, own, 1, 3, at(space, across))
    sized(pooled.at[0, 0, pl.ds(0, 3)], sems.at[3]).wait()
    for step in range(4):
        beside = group * 4 + (rest + step) % 4
        give(
            pooled.at[1, rest], pooled.at[near, rest], 4, 5, at(space + 1 - 2 * core, beside)
        )
        if step:
            give(pooled.at[1, rest], pooled.at[1, rest], 6, 7, at(space, beside))

    @pl.when(has_side)
    def _():
        sized(pooled.at[0, 0], sems.at[2]).wait()
        for step in range(1, 4):
            beside = group * 4 + (rest + step) % 4
            give(pooled.at[near, rest], pooled.at[near, rest], 8, 9, at(space, beside))
        sized(pooled.at[0, pl.ds(0, 3)], sems.at[9]).wait()

    sized(pooled.at[0], sems.at[5]).wait()
    sized(pooled.at[0, pl.ds(0, 3)], sems.at[7]).wait()

    lanes = lax.broadcasted_iota(jnp.int32, (32, 128), 1)
    for a in range(3):
        for pair in range(8):
            rows = [
                pooled[a, row % 4, row // 4].astype(jnp.float32) for row in (2 * pair, 2 * pair + 1)
            ]
            low = jnp.where(lanes < 64, rows[0], pltpu.roll(rows[1], 64, 1))
            top = jnp.where(lanes < 64, pltpu.roll(rows[0], 64, 1), rows[1])
            grid[pl.ds(a * 64, 32), pl.ds(pair * 128, 128)] = low.astype(jnp.bfloat16)
            grid[pl.ds(a * 64 + 32, 32), pl.ds(pair * 128, 128)] = top.astype(jnp.bfloat16)

    products[...] = dot(deep_mat[...], grid[...])
    column = lax.broadcasted_iota(jnp.int32, (32, CELLS), 1)
    depth = column % 64

    def tap(b, c):
        return products[pl.ds((b * 3 + c) * 32, 32), :]

    def line(b):
        return (
            tap(b, 1)
            + jnp.where(depth == 0, 0.0, pltpu.roll(tap(b, 0), 1, 1))
            + jnp.where(depth == 63, 0.0, pltpu.roll(tap(b, 2), CELLS - 1, 1))
        )

    pre = line(1)
    pre = pre + jnp.where(column < 64, 0.0, pltpu.roll(line(0), 64, 1))
    pre = pre + jnp.where(column >= CELLS - 64, 0.0, pltpu.roll(line(2), CELLS - 64, 1))
    sigma = 1.0 / (1.0 + jnp.exp(-pre))
    out_ref[...] = (pre * sigma).astype(jnp.bfloat16)
    grad_pre = cot[...].astype(jnp.float32) * sigma * (1.0 + pre * (1.0 - sigma))
    grad_pre = grad_pre.astype(jnp.bfloat16).astype(jnp.float32)
    for b in range(3):
        for c in range(3):
            keep = grad_pre
            if b == 0:
                keep = jnp.where(column < 64, 0.0, keep)
            if b == 2:
                keep = jnp.where(column >= CELLS - 64, 0.0, keep)
            if c == 0:
                keep = jnp.where(depth == 0, 0.0, keep)
            if c == 2:
                keep = jnp.where(depth == 63, 0.0, keep)
            shift = ((b - 1) * 64 + c - 1) % CELLS
            if shift:
                keep = pltpu.roll(keep, shift, 1)
            shifted[pl.ds((b * 3 + c) * 32, 32), :] = keep.astype(jnp.bfloat16)
    local = lax.dot_general(
        shifted[...], grid[...], (((1,), (1,)), ((), ())), preferred_element_type=jnp.float32
    )
    terms[pl.ds(0, 18)] = local[:, 0:128].reshape(18, 16, 128)
    last = jnp.concatenate([local[0:144, 128:192], local[144:288, 128:192]], axis=1)
    terms[pl.ds(18, 9)] = last.reshape(9, 16, 128)

    owner = here < CHUNKS
    for step in range(1, PLANE):
        to = peer(step)

        @pl.when(to < CHUNKS)
        def _():
            give(terms.at[to], parts.at[here], 10, 11, at(place(to, high), chan))

    @pl.when(owner)
    def _():
        parts[here] = terms[here]
        sized(parts.at[pl.ds(0, PLANE - 1)], sems.at[11]).wait()
        mine[...] = jnp.sum(parts[...], axis=0)
        swap = pltpu.make_async_remote_copy(
            mine, far, sems.at[12], sems.at[13], device_id=at(other, chan), device_id_type=MESH
        )
        swap.start()
        swap.wait()
        sums[here] = mine[...] + far[...]
        for step in range(1, PLANE):
            give(sums.at[here], sums.at[here], 14, 15, at(place(peer(step), high), chan))
        sized(sums.at[pl.ds(0, CHUNKS - 1)], sems.at[15]).wait()
        sized(parts.at[pl.ds(0, PLANE - 1)], sems.at[14]).wait()
        sized(terms.at[pl.ds(0, CHUNKS - 1)], sems.at[10]).wait()

    @pl.when(jnp.logical_not(owner))
    def _():
        sized(sums, sems.at[15]).wait()
        sized(terms, sems.at[10]).wait()

    for block in range(18):
        b, c, half = block // 6, (block // 2) % 3, block % 2
        rows = pl.ds(half * 16, 16)
        both = sums[block]
        grad_ref[0, b, c, rows, :] = both[:, 0:64]
        grad_ref[1, b, c, rows, :] = both[:, 64:128]
        third = sums[18 + block % 9]
        grad_ref[2, b, c, rows, :] = third[:, 0:64] if block < 9 else third[:, 64:128]

    @pl.when(has_side)
    def _():
        sized(pooled.at[0, 0], sems.at[0]).wait()
        sized(pooled.at[0, pl.ds(0, 3)], sems.at[8]).wait()

    sized(pooled.at[0, 0, pl.ds(0, 3)], sems.at[1]).wait()
    sized(pooled.at[0], sems.at[4]).wait()
    sized(pooled.at[0, pl.ds(0, 3)], sems.at[6]).wait()


def on_device(volume, weight_first, weight_deep, cotangent):
    bf16, f32 = jnp.bfloat16, jnp.float32
    deep_out, grad_deep = pl.pallas_call(
        step_kernel,
        out_shape=(
            jax.ShapeDtypeStruct((32, CELLS), bf16),
            jax.ShapeDtypeStruct((3, 3, 3, 32, 64), f32),
        ),
        in_specs=[pl.BlockSpec(memory_space=pl.ANY)] * 4,
        out_specs=(
            pl.BlockSpec(memory_space=pltpu.VMEM),
            pl.BlockSpec(memory_space=pltpu.VMEM),
        ),
        scratch_shapes=[
            pltpu.VMEM((4, 4, 32, 128), bf16),
            pltpu.VMEM((3, 3, 3, 32, 64), bf16),
            pltpu.VMEM((3, 3, 3, 32, 64), bf16),
            pltpu.VMEM((32, CELLS), bf16),
            pltpu.VMEM((288, 192), bf16),
            pltpu.VMEM((288, 192), bf16),
            pltpu.VMEM((288, 512), bf16),
            pltpu.VMEM((3, 4, 4, 32, 128), bf16),
            pltpu.VMEM((192, CELLS), bf16),
            pltpu.VMEM((288, CELLS), f32),
            pltpu.VMEM((288, CELLS), bf16),
            pltpu.VMEM((CHUNKS, 16, 128), f32),
            pltpu.VMEM((PLANE, 16, 128), f32),
            pltpu.VMEM((16, 128), f32),
            pltpu.VMEM((16, 128), f32),
            pltpu.VMEM((CHUNKS, 16, 128), f32),
            pltpu.SemaphoreType.DMA((4,)),
            pltpu.SemaphoreType.DMA((8,)),
            pltpu.SemaphoreType.DMA((8,)),
            pltpu.SemaphoreType.DMA((16,)),
        ],
        compiler_params=pltpu.CompilerParams(
            collective_id=0, has_side_effects=True, vmem_limit_bytes=32 * 2**20
        ),
        name="step",
    )(
        jnp.transpose(volume, (1, 2, 0, 3)),
        jnp.transpose(weight_first, (0, 1, 2, 4, 3)),
        weight_deep,
        cotangent.reshape(32, CELLS),
    )
    return deep_out.reshape(32, 1, CELLS), grad_deep


def solution(mesh):
    return jax.shard_map(
        on_device,
        mesh=mesh,
        in_specs=(
            P(None, "space", "chan", None),
            P(),
            P(None, None, None, "chan", None),
            P("chan", "space", None),
        ),
        out_specs=(P("chan", "space", None), P(None, None, None, "chan", None)),
        check_vma=False,
    )
```

```python
import jax
import jax.numpy as jnp
from jax import lax
from jax.experimental import pallas as pl
from jax.experimental.pallas import tpu as pltpu
from jax.sharding import PartitionSpec as P

MESH = pl.DeviceIdType.MESH
CHUNKS = 27
PLANE = 32
SPACE = 64
CHAN = 16
CELLS = 1024
OFFSETS = sorted(
    [(i, j, k) for i in range(4) for j in range(4) for k in range(2) if (i, j, k) != (0, 0, 0)],
    key=lambda o: (-min(o[0], 4 - o[0]) - min(o[1], 4 - o[1]), o),
)
SIDES = [(dx, dy) for dx in (-1, 0, 1) for dy in (-1, 0, 1) if (dx, dy) != (0, 0)]
SOURCE = {-1: 1, 0: pl.ds(1, 2), 1: 2}
TARGET = {-1: 3, 0: pl.ds(1, 2), 1: 0}


def at(space, chan):
    return {"space": space, "chan": chan}


def sized(ref, sem):
    return pltpu.make_async_copy(ref, ref, sem)


def dot(left, right):
    return jnp.dot(left, right, preferred_element_type=jnp.float32)


def step_kernel(
    vol_in, first_in, deep_in, cot_in, out_ref, grad_ref,
    slab, relay, first, deep, cot, first_mat, deep_mat, windows,
    pooled, grid, products, shifted, terms, parts, mine, far, sums,
    local_sems, halo_send, halo_recv, sems,
):
    space = lax.axis_index("space")
    chan = lax.axis_index("chan")
    core = space % 2
    high = (space // 8) % 2
    line, row = space // 16, (space // 2) % 4
    here = line * 8 + row * 2 + core
    other = space + 8 - 16 * high
    rest = chan % 4
    group = chan // 4
    side = space - 1 + 2 * core
    has_side = (side >= 0) & (side < SPACE)
    near, away = 2 * core, 2 - 2 * core

    lines = [(line + step) % 4 for step in range(4)]
    rows = [(row + step) % 4 for step in range(4)]
    cores = [core, 1 - core]
    peers = [
        (lines[i] * 16 + high * 8 + rows[j] * 2 + cores[k], lines[i] * 8 + rows[j] * 2 + cores[k])
        for i, j, k in OFFSETS
    ]
    edge = space % 8
    crossing = has_side & ((edge == 0) | (edge == 7))
    straight = has_side & (edge != 0) & (edge != 7)

    def exists(dx, dy):
        x, y = space + dx, chan + dy
        inside = (x >= 0) & (x < SPACE) & (y >= 0) & (y < CHAN)
        if dx == 0:
            return inside
        return inside & (edge != (7 if dx == 1 else 0))

    def give(src, dst, send, recv, device):
        pltpu.make_async_remote_copy(
            src, dst, sems.at[send], sems.at[recv], device_id=device, device_id_type=MESH
        ).start()

    acrosses = [(group + step) % 4 * 4 + rest for step in range(4)]
    besides = [group * 4 + (rest + step) % 4 for step in range(4)]
    loads = [
        pltpu.make_async_copy(src, dst, local_sems.at[i])
        for i, (src, dst) in enumerate(
            [
                (vol_in, slab.at[pl.ds(1, 2), pl.ds(1, 2)]),
                (first_in, first),
                (deep_in, deep),
                (cot_in, cot),
            ]
        )
    ]
    for load in loads:
        load.start()

    barrier = pltpu.get_barrier_semaphore()

    def hello(device):
        pl.semaphore_signal(barrier, inc=1, device_id=device, device_id_type=MESH)

    opposite = (chan + 8) % CHAN
    expected = PLANE - 1 + 6 + jnp.where(straight, 3, 0)
    for dy in (0, -1, 1):
        meets = crossing & (chan + dy >= 0) & (chan + dy < CHAN)
        met = crossing & (opposite + dy >= 0) & (opposite + dy < CHAN)
        expected = expected + jnp.where(met, 1, 0)

        @pl.when(meets)
        def _():
            hello(at(side, (chan + dy + 8) % CHAN))

    for dx, dy in SIDES:
        here_too = exists(dx, dy)
        expected = expected + jnp.where(here_too, 1, 0)

        @pl.when(here_too)
        def _():
            hello(at(space + dx, chan + dy))

    for across in acrosses[1:]:
        hello(at(space, across))
    for beside in besides[1:]:
        hello(at(space, beside))

    @pl.when(straight)
    def _():
        for across in acrosses[1:]:
            hello(at(side, across))

    for device, _ in peers:
        hello(at(device, chan))

    @pl.when(space == 0)
    def _():
        slab[0] = jnp.zeros_like(slab[0])
        pooled[0] = jnp.zeros_like(pooled[0])

    @pl.when(space == SPACE - 1)
    def _():
        slab[3] = jnp.zeros_like(slab[3])
        pooled[2] = jnp.zeros_like(pooled[2])

    @pl.when(chan == 0)
    def _():
        slab[:, 0] = jnp.zeros_like(slab[:, 0])

    @pl.when(chan == CHAN - 1)
    def _():
        slab[:, 3] = jnp.zeros_like(slab[:, 3])

    loads[0].wait()
    pl.semaphore_wait(barrier, expected)

    def rim(n):
        dx, dy = SIDES[n]
        return pltpu.make_async_remote_copy(
            slab.at[SOURCE[dx], SOURCE[dy]],
            slab.at[TARGET[dx], TARGET[dy]],
            halo_send.at[n],
            halo_recv.at[n],
            device_id=at(space + dx, chan + dy),
            device_id_type=MESH,
        )

    for n, (dx, dy) in enumerate(SIDES):

        @pl.when(exists(dx, dy))
        def _():
            rim(n).start()

    ahead, behind = 1 + core, 3 * core
    face = slab.at[ahead, pl.ds(1, 2)]

    @pl.when(crossing)
    def _():
        give(face, relay, 19, 20, at(space, opposite))

    for load in loads[1:]:
        load.wait()
    for a in range(3):
        for b in range(3):
            for c in range(3):
                first_mat[pl.ds((a * 3 + b) * 32, 32), pl.ds(c * 64, 64)] = first[a, b, c]
                deep_mat[pl.ds((b * 3 + c) * 32, 32), pl.ds(a * 64, 64)] = deep[a, b, c]

    for n, (dx, dy) in enumerate(SIDES):

        @pl.when(exists(-dx, -dy))
        def _():
            ref = slab.at[TARGET[dx], TARGET[dy]]
            sized(ref, halo_recv.at[n]).wait()

    for n, (dx, dy) in enumerate(SIDES):

        @pl.when(exists(dx, dy))
        def _():
            ref = slab.at[SOURCE[dx], SOURCE[dy]]
            sized(ref, halo_send.at[n]).wait()

    @pl.when(crossing)
    def _():
        sized(relay, sems.at[20]).wait()
        give(relay, slab.at[3 - behind, pl.ds(1, 2)], 21, 22, at(side, opposite))

        @pl.when(opposite > 0)
        def _():
            give(relay.at[0], slab.at[3 - behind, 3], 23, 24, at(side, opposite - 1))

        @pl.when(opposite < CHAN - 1)
        def _():
            give(relay.at[1], slab.at[3 - behind, 0], 25, 26, at(side, opposite + 1))

        sized(relay, sems.at[22]).wait()

        @pl.when(chan < CHAN - 1)
        def _():
            sized(relay.at[0], sems.at[24]).wait()

        @pl.when(chan > 0)
        def _():
            sized(relay.at[0], sems.at[26]).wait()

    for x in range(2):
        for y in range(2):
            for a in range(3):
                for b in range(3):
                    windows[pl.ds((a * 3 + b) * 32, 32), pl.ds((x * 2 + y) * 128, 128)] = slab[
                        x + a, y + b
                    ]
    taps = lax.dot_general(
        first_mat[...], windows[...], (((0,), (0,)), ((), ())), preferred_element_type=jnp.float32
    )
    z = lax.broadcasted_iota(jnp.int32, (64, 512), 1) % 128
    pre = taps[64:128]
    pre = pre + jnp.where(z == 0, 0.0, pltpu.roll(taps[0:64], 1, 1))
    pre = pre + jnp.where(z == 127, 0.0, pltpu.roll(taps[128:192], 511, 1))
    act = pre / (1.0 + jnp.exp(-pre))
    added = act[:, 0:128] + act[:, 128:256] + act[:, 256:384] + act[:, 384:512]
    mean = ((added + pltpu.roll(added, 127, 1)) * 0.125).astype(jnp.bfloat16)
    lane = lax.broadcasted_iota(jnp.int32, (128, 128), 0)
    cell = lax.broadcasted_iota(jnp.int32, (128, 128), 1)
    left = jnp.where(lane == 2 * cell, 1.0, 0.0).astype(jnp.bfloat16)
    right = jnp.where(lane == 2 * cell - 128, 1.0, 0.0).astype(jnp.bfloat16)
    piece = dot(mean[0:32], left) + dot(mean[32:64], right)
    pooled[1, rest, group] = piece.astype(jnp.bfloat16)

    own = pooled.at[1, rest, group]

    for across in acrosses[1:]:
        give(own, own, 1, 3, at(space, across))

    @pl.when(has_side)
    def _():
        for across in acrosses:
            give(own, pooled.at[away, rest, group], 0, 2, at(side, across))

    sibling = at(space + 1 - 2 * core, chan)
    sized(pooled.at[0, 0, pl.ds(0, 3)], sems.at[3]).wait()
    for step in (3, 2, 1):
        give(pooled.at[1, rest], pooled.at[1, rest], 6, 15 + step, at(space, besides[step]))
    give(pooled.at[1, rest], pooled.at[near, rest], 4, 5, sibling)

    @pl.when(has_side)
    def _():
        sized(pooled.at[0, 0], sems.at[2]).wait()
        for step in (3, 2, 1):
            give(pooled.at[near, rest], pooled.at[near, rest], 8, 9, at(space, besides[step]))

    for step in (1, 2, 3):
        sized(pooled.at[0, 0], sems.at[15 + step]).wait()
        block = (rest + 4 - step) % 4
        give(pooled.at[1, block], pooled.at[near, block], 4, 5, sibling)

    @pl.when(has_side)
    def _():
        sized(pooled.at[0, pl.ds(0, 3)], sems.at[9]).wait()

    sized(pooled.at[0], sems.at[5]).wait()

    lanes = lax.broadcasted_iota(jnp.int32, (32, 128), 1)
    for a in range(3):
        for pair in range(8):
            rows = [
                pooled[a, row % 4, row // 4].astype(jnp.float32) for row in (2 * pair, 2 * pair + 1)
            ]
            low = jnp.where(lanes < 64, rows[0], pltpu.roll(rows[1], 64, 1))
            top = jnp.where(lanes < 64, pltpu.roll(rows[0], 64, 1), rows[1])
            grid[pl.ds(a * 64, 32), pl.ds(pair * 128, 128)] = low.astype(jnp.bfloat16)
            grid[pl.ds(a * 64 + 32, 32), pl.ds(pair * 128, 128)] = top.astype(jnp.bfloat16)

    products[...] = dot(deep_mat[...], grid[...])
    column = lax.broadcasted_iota(jnp.int32, (32, CELLS), 1)
    depth = column % 64

    def tap(b, c):
        return products[pl.ds((b * 3 + c) * 32, 32), :]

    def line(b):
        return (
            tap(b, 1)
            + jnp.where(depth == 0, 0.0, pltpu.roll(tap(b, 0), 1, 1))
            + jnp.where(depth == 63, 0.0, pltpu.roll(tap(b, 2), CELLS - 1, 1))
        )

    pre = line(1)
    pre = pre + jnp.where(column < 64, 0.0, pltpu.roll(line(0), 64, 1))
    pre = pre + jnp.where(column >= CELLS - 64, 0.0, pltpu.roll(line(2), CELLS - 64, 1))
    sigma = 1.0 / (1.0 + jnp.exp(-pre))
    out_ref[...] = (pre * sigma).astype(jnp.bfloat16)
    grad_pre = cot[...].astype(jnp.float32) * sigma * (1.0 + pre * (1.0 - sigma))
    grad_pre = grad_pre.astype(jnp.bfloat16).astype(jnp.float32)
    for b in range(3):
        for c in range(3):
            keep = grad_pre
            if b == 0:
                keep = jnp.where(column < 64, 0.0, keep)
            if b == 2:
                keep = jnp.where(column >= CELLS - 64, 0.0, keep)
            if c == 0:
                keep = jnp.where(depth == 0, 0.0, keep)
            if c == 2:
                keep = jnp.where(depth == 63, 0.0, keep)
            shift = ((b - 1) * 64 + c - 1) % CELLS
            if shift:
                keep = pltpu.roll(keep, shift, 1)
            shifted[pl.ds((b * 3 + c) * 32, 32), :] = keep.astype(jnp.bfloat16)
    local = lax.dot_general(
        shifted[...], grid[...], (((1,), (1,)), ((), ())), preferred_element_type=jnp.float32
    )
    terms[pl.ds(0, 18)] = local[:, 0:128].reshape(18, 16, 128)
    last = jnp.concatenate([local[0:144, 128:192], local[144:288, 128:192]], axis=1)
    terms[pl.ds(18, 9)] = last.reshape(9, 16, 128)

    owner = here < CHUNKS
    for device, to in peers:

        @pl.when(to < CHUNKS)
        def _():
            give(terms.at[to], parts.at[here], 10, 11, at(device, chan))

    @pl.when(owner)
    def _():
        parts[here] = terms[here]
        sized(parts.at[pl.ds(0, PLANE - 1)], sems.at[11]).wait()
        mine[...] = jnp.sum(parts[...], axis=0)
        swap = pltpu.make_async_remote_copy(
            mine, far, sems.at[12], sems.at[13], device_id=at(other, chan), device_id_type=MESH
        )
        swap.start()
        swap.wait()
        sums[here] = (mine[...] + far[...]).astype(jnp.bfloat16)
        for device, _ in peers:
            give(sums.at[here], sums.at[here], 14, 15, at(device, chan))
        sized(sums.at[pl.ds(0, CHUNKS - 1)], sems.at[15]).wait()
        sized(sums.at[pl.ds(0, PLANE - 1)], sems.at[14]).wait()
        sized(terms.at[pl.ds(0, CHUNKS - 1)], sems.at[10]).wait()

    @pl.when(jnp.logical_not(owner))
    def _():
        sized(sums.at[pl.ds(0, CHUNKS)], sems.at[15]).wait()
        sized(terms, sems.at[10]).wait()

    for block in range(18):
        b, c, half = block // 6, (block // 2) % 3, block % 2
        part = pl.ds(half * 16, 16)
        both = sums[block].astype(jnp.float32)
        grad_ref[0, b, c, part, :] = both[:, 0:64]
        grad_ref[1, b, c, part, :] = both[:, 64:128]
        third = sums[18 + block % 9].astype(jnp.float32)
        grad_ref[2, b, c, part, :] = third[:, 0:64] if block < 9 else third[:, 64:128]

    @pl.when(crossing)
    def _():
        sized(relay, sems.at[19]).wait()
        sized(relay, sems.at[21]).wait()

        @pl.when(opposite > 0)
        def _():
            sized(relay.at[0], sems.at[23]).wait()

        @pl.when(opposite < CHAN - 1)
        def _():
            sized(relay.at[0], sems.at[25]).wait()

    @pl.when(has_side)
    def _():
        sized(pooled.at[0, 0], sems.at[0]).wait()
        sized(pooled.at[0, pl.ds(0, 3)], sems.at[8]).wait()

    sized(pooled.at[0, 0, pl.ds(0, 3)], sems.at[1]).wait()
    sized(pooled.at[0], sems.at[4]).wait()
    sized(pooled.at[0, pl.ds(0, 3)], sems.at[6]).wait()


def on_device(volume, weight_first, weight_deep, cotangent):
    bf16, f32 = jnp.bfloat16, jnp.float32
    deep_out, grad_deep = pl.pallas_call(
        step_kernel,
        out_shape=(
            jax.ShapeDtypeStruct((32, CELLS), bf16),
            jax.ShapeDtypeStruct((3, 3, 3, 32, 64), f32),
        ),
        in_specs=[pl.BlockSpec(memory_space=pl.ANY)]
        + [pl.BlockSpec(memory_space=pltpu.HBM)] * 3,
        out_specs=(
            pl.BlockSpec(memory_space=pltpu.VMEM),
            pl.BlockSpec(memory_space=pltpu.VMEM),
        ),
        scratch_shapes=[
            pltpu.VMEM((4, 4, 32, 128), bf16),
            pltpu.VMEM((2, 32, 128), bf16),
            pltpu.VMEM((3, 3, 3, 32, 64), bf16),
            pltpu.VMEM((3, 3, 3, 32, 64), bf16),
            pltpu.VMEM((32, CELLS), bf16),
            pltpu.VMEM((288, 192), bf16),
            pltpu.VMEM((288, 192), bf16),
            pltpu.VMEM((288, 512), bf16),
            pltpu.VMEM((3, 4, 4, 32, 128), bf16),
            pltpu.VMEM((192, CELLS), bf16),
            pltpu.VMEM((288, CELLS), f32),
            pltpu.VMEM((288, CELLS), bf16),
            pltpu.VMEM((CHUNKS, 16, 128), f32),
            pltpu.VMEM((PLANE, 16, 128), f32),
            pltpu.VMEM((16, 128), f32),
            pltpu.VMEM((16, 128), f32),
            pltpu.VMEM((PLANE, 16, 128), bf16),
            pltpu.SemaphoreType.DMA((4,)),
            pltpu.SemaphoreType.DMA((8,)),
            pltpu.SemaphoreType.DMA((8,)),
            pltpu.SemaphoreType.DMA((27,)),
        ],
        compiler_params=pltpu.CompilerParams(
            collective_id=0, has_side_effects=True, vmem_limit_bytes=32 * 2**20
        ),
        name="step",
    )(
        jnp.transpose(volume, (1, 2, 0, 3)),
        jnp.transpose(weight_first, (0, 1, 2, 4, 3)),
        weight_deep,
        cotangent.reshape(32, CELLS),
    )
    return deep_out.reshape(32, 1, CELLS), grad_deep


def solution(mesh):
    return jax.shard_map(
        on_device,
        mesh=mesh,
        in_specs=(
            P(None, "space", "chan", None),
            P(),
            P(None, None, None, "chan", None),
            P("chan", "space", None),
        ),
        out_specs=(P("chan", "space", None), P(None, None, None, "chan", None)),
        check_vma=False,
    )
```

```python
import jax
import jax.numpy as jnp
from jax import lax
from jax.experimental import pallas as pl
from jax.experimental.pallas import tpu as pltpu
from jax.sharding import PartitionSpec as P

MESH = pl.DeviceIdType.MESH
CHUNKS = 27
PLANE = 32
SPACE = 64
CHAN = 16
CELLS = 1024
OFFSETS = sorted(
    [(i, j, k) for i in range(4) for j in range(4) for k in range(2) if (i, j, k) != (0, 0, 0)],
    key=lambda o: (-min(o[0], 4 - o[0]) - min(o[1], 4 - o[1]), o),
)
SIDES = [(dx, dy) for dx in (-1, 0, 1) for dy in (-1, 0, 1) if (dx, dy) != (0, 0)]
SOURCE = {-1: 1, 0: pl.ds(1, 2), 1: 2}
TARGET = {-1: 3, 0: pl.ds(1, 2), 1: 0}


def at(space, chan):
    return {"space": space, "chan": chan}


def sized(ref, sem):
    return pltpu.make_async_copy(ref, ref, sem)


def dot(left, right):
    return jnp.dot(left, right, preferred_element_type=jnp.float32)


def step_kernel(
    vol_in, first_in, deep_in, cot_in, out_ref, grad_ref,
    slab, relay, first, deep, cot, first_mat, deep_mat, windows,
    pooled, grid, products, shifted, terms, parts, mine, far, sums,
    local_sems, halo_send, halo_recv, sems, wide, ready, go, plane,
):
    space = lax.axis_index("space")
    chan = lax.axis_index("chan")
    core = space % 2
    high = (space // 8) % 2
    line, row = space // 16, (space // 2) % 4
    here = line * 8 + row * 2 + core
    other = space + 8 - 16 * high
    rest = chan % 4
    group = chan // 4
    side = space - 1 + 2 * core
    has_side = (side >= 0) & (side < SPACE)
    near, away = 2 * core, 2 - 2 * core

    lines = [(line + step) % 4 for step in range(4)]
    rows = [(row + step) % 4 for step in range(4)]
    cores = [core, 1 - core]
    peers = [
        (lines[i] * 16 + high * 8 + rows[j] * 2 + cores[k], lines[i] * 8 + rows[j] * 2 + cores[k])
        for i, j, k in OFFSETS
    ]
    edge = space % 8
    crossing = has_side & ((edge == 0) | (edge == 7))
    straight = has_side & (edge != 0) & (edge != 7)

    def exists(dx, dy):
        x, y = space + dx, chan + dy
        inside = (x >= 0) & (x < SPACE) & (y >= 0) & (y < CHAN)
        if dx == 0:
            return inside
        return inside & (edge != (7 if dx == 1 else 0))

    def give(src, dst, send, recv, device):
        pltpu.make_async_remote_copy(
            src, dst, sems.at[send], sems.at[recv], device_id=device, device_id_type=MESH
        ).start()

    low = 1 - group // 2
    spots = [group, low * (1 - group) + (1 - low) * (5 - group), 1 + low, 3 * low]
    besides = [group * 4 + (rest + step) % 4 for step in range(4)]
    loads = [
        pltpu.make_async_copy(src, dst, local_sems.at[i])
        for i, (src, dst) in enumerate(
            [
                (vol_in, slab.at[pl.ds(1, 2), pl.ds(1, 2)]),
                (first_in, first),
                (deep_in, deep),
                (cot_in, cot),
            ]
        )
    ]
    for load in loads:
        load.start()

    barrier = pltpu.get_barrier_semaphore()

    def hello(device):
        pl.semaphore_signal(barrier, inc=1, device_id=device, device_id_type=MESH)

    helper = ((edge == 2) & (space > 2)) | ((edge == 5) & (space < SPACE - 3))
    opposite = (chan + 8) % CHAN
    outer = (group == 0) | (group == 3)
    expected = 10 + 3
    for dy in (0, -1, 1):
        meets = crossing & (chan + dy >= 0) & (chan + dy < CHAN)
        met = helper & (opposite + dy >= 0) & (opposite + dy < CHAN)
        expected = expected + jnp.where(met, 1, 0)

        @pl.when(meets)
        def _():
            hello(at(side - 2 + 4 * core, (chan + dy + 8) % CHAN))

    for dx, dy in SIDES:
        here_too = exists(dx, dy)
        expected = expected + jnp.where(here_too, 1, 0)

        @pl.when(here_too)
        def _():
            hello(at(space + dx, chan + dy))

    for n in range(3):
        close = n < 2 or jnp.logical_not(outer)
        expected = expected + jnp.where(close, 1, 0) + jnp.where(straight & close, 1, 0)

        @pl.when(close)
        def _():
            hello(at(space, spots[n + 1] * 4 + rest))

        @pl.when(straight & close)
        def _():
            hello(at(side, spots[n + 1] * 4 + rest))

    for beside in besides[1:]:
        hello(at(space, beside))

    column = [at(line * 16 + high * 8 + rows[j] * 2 + core, chan) for j in range(1, 4)]
    hello(at(space + 1 - 2 * core, chan))
    for i in range(1, 4):
        for k in range(2):
            hello(at(lines[i] * 16 + high * 8 + row * 2 + cores[k], chan))
    for device in column:
        hello(device)

    @pl.when(space == 0)
    def _():
        slab[0] = jnp.zeros_like(slab[0])
        pooled[0] = jnp.zeros_like(pooled[0])

    @pl.when(space == SPACE - 1)
    def _():
        slab[3] = jnp.zeros_like(slab[3])
        pooled[2] = jnp.zeros_like(pooled[2])

    @pl.when(chan == 0)
    def _():
        slab[:, 0] = jnp.zeros_like(slab[:, 0])

    @pl.when(chan == CHAN - 1)
    def _():
        slab[:, 3] = jnp.zeros_like(slab[:, 3])

    loads[0].wait()
    pl.semaphore_wait(barrier, expected)
    pl.semaphore_signal(ready, inc=1, device_id=at(space, opposite), device_id_type=MESH)

    for device in column:
        pl.semaphore_signal(plane, inc=1, device_id=device, device_id_type=MESH)

    @pl.when(helper)
    def _():
        relayed = at(space - 2 + 4 * core, chan)
        pl.semaphore_signal(go, inc=1, device_id=relayed, device_id_type=MESH)

    def rim(n):
        dx, dy = SIDES[n]
        return pltpu.make_async_remote_copy(
            slab.at[SOURCE[dx], SOURCE[dy]],
            slab.at[TARGET[dx], TARGET[dy]],
            halo_send.at[n],
            halo_recv.at[n],
            device_id=at(space + dx, chan + dy),
            device_id_type=MESH,
        )

    for n, (dx, dy) in enumerate(SIDES):

        @pl.when(exists(dx, dy))
        def _():
            rim(n).start()

    ahead, behind = 1 + core, 3 * core
    face = slab.at[ahead, pl.ds(1, 2)]

    @pl.when(crossing)
    def _():
        give(face, relay, 19, 20, at(space, opposite))

    for load in loads[1:]:
        load.wait()
    for a in range(3):
        for b in range(3):
            for c in range(3):
                first_mat[pl.ds((a * 3 + b) * 32, 32), pl.ds(c * 64, 64)] = first[a, b, c]
                deep_mat[pl.ds((b * 3 + c) * 32, 32), pl.ds(a * 64, 64)] = deep[a, b, c]

    for n, (dx, dy) in enumerate(SIDES):

        @pl.when(exists(-dx, -dy))
        def _():
            ref = slab.at[TARGET[dx], TARGET[dy]]
            sized(ref, halo_recv.at[n]).wait()

    for n, (dx, dy) in enumerate(SIDES):

        @pl.when(exists(dx, dy))
        def _():
            ref = slab.at[SOURCE[dx], SOURCE[dy]]
            sized(ref, halo_send.at[n]).wait()

    @pl.when(crossing)
    def _():
        sized(relay, sems.at[20]).wait()
        pl.semaphore_wait(go, 1)
        give(relay, slab.at[3 - behind, pl.ds(1, 2)], 21, 22, at(side, opposite))

        @pl.when(opposite > 0)
        def _():
            give(relay.at[0], slab.at[3 - behind, 3], 23, 24, at(side, opposite - 1))

        @pl.when(opposite < CHAN - 1)
        def _():
            give(relay.at[1], slab.at[3 - behind, 0], 25, 26, at(side, opposite + 1))

        sized(relay, sems.at[22]).wait()

        @pl.when(chan < CHAN - 1)
        def _():
            sized(relay.at[0], sems.at[24]).wait()

        @pl.when(chan > 0)
        def _():
            sized(relay.at[0], sems.at[26]).wait()

    for x in range(2):
        for y in range(2):
            for a in range(3):
                for b in range(3):
                    windows[pl.ds((a * 3 + b) * 32, 32), pl.ds((x * 2 + y) * 128, 128)] = slab[
                        x + a, y + b
                    ]
    taps = lax.dot_general(
        first_mat[...], windows[...], (((0,), (0,)), ((), ())), preferred_element_type=jnp.float32
    )
    z = lax.broadcasted_iota(jnp.int32, (64, 512), 1) % 128
    pre = taps[64:128]
    pre = pre + jnp.where(z == 0, 0.0, pltpu.roll(taps[0:64], 1, 1))
    pre = pre + jnp.where(z == 127, 0.0, pltpu.roll(taps[128:192], 511, 1))
    act = pre / (1.0 + jnp.exp(-pre))
    added = act[:, 0:128] + act[:, 128:256] + act[:, 256:384] + act[:, 384:512]
    mean = ((added + pltpu.roll(added, 127, 1)) * 0.125).astype(jnp.bfloat16)
    lane = lax.broadcasted_iota(jnp.int32, (128, 128), 0)
    cell = lax.broadcasted_iota(jnp.int32, (128, 128), 1)
    left = jnp.where(lane == 2 * cell, 1.0, 0.0).astype(jnp.bfloat16)
    right = jnp.where(lane == 2 * cell - 128, 1.0, 0.0).astype(jnp.bfloat16)
    piece = dot(mean[0:32], left) + dot(mean[32:64], right)
    pooled[1, rest, group] = piece.astype(jnp.bfloat16)

    own = pooled.at[1, rest, group]
    sibling = at(space + 1 - 2 * core, chan)
    flip = jnp.where(crossing, 1, 0)
    turns = [spots[n] + flip * (spots[3 - n] - spots[n]) for n in range(4)]

    def to_mates(plane, index, send, recv):
        for step in (3, 2, 1):
            piece = pooled.at[plane, rest, index]
            give(piece, piece, send, recv, at(space, besides[step]))

    def own_row(n):
        if n:
            sized(own, wide.at[spots[n]]).wait()
        to_mates(1, spots[n], 6, 27 + n)

    def side_row(n):
        @pl.when(has_side)
        def _():
            sized(own, wide.at[4 + turns[n]]).wait()
            to_mates(near, turns[n], 8, 9)

    def to_sibling(n):
        sized(pooled.at[0, 0, pl.ds(0, 3)], sems.at[27 + n]).wait()
        give(pooled.at[1, :, spots[n]], pooled.at[near, :, spots[n]], 4, 5, sibling)

    pl.semaphore_wait(ready, 1)
    pl.semaphore_wait(plane, 3)
    for n in (3, 2, 1):
        pltpu.make_async_remote_copy(
            own, own, sems.at[1], wide.at[group],
            device_id=at(space, spots[n] * 4 + rest), device_id_type=MESH,
        ).start()

    @pl.when(has_side)
    def _():
        for n in (3, 2, 1, 0):
            pltpu.make_async_remote_copy(
                own, pooled.at[away, rest, group], sems.at[0], wide.at[4 + group],
                device_id=at(side, spots[n] * 4 + rest), device_id_type=MESH,
            ).start()

    own_row(0)
    for n in range(1, 4):
        side_row(n - 1)
        own_row(n)
        to_sibling(n - 1)
    side_row(3)
    to_sibling(3)

    @pl.when(has_side)
    def _():
        sized(pooled.at[0, pl.ds(0, 3)], sems.at[9]).wait()

    sized(pooled.at[0], sems.at[5]).wait()

    lanes = lax.broadcasted_iota(jnp.int32, (32, 128), 1)
    for a in range(3):
        for pair in range(8):
            rows = [
                pooled[a, row % 4, row // 4].astype(jnp.float32) for row in (2 * pair, 2 * pair + 1)
            ]
            low = jnp.where(lanes < 64, rows[0], pltpu.roll(rows[1], 64, 1))
            top = jnp.where(lanes < 64, pltpu.roll(rows[0], 64, 1), rows[1])
            grid[pl.ds(a * 64, 32), pl.ds(pair * 128, 128)] = low.astype(jnp.bfloat16)
            grid[pl.ds(a * 64 + 32, 32), pl.ds(pair * 128, 128)] = top.astype(jnp.bfloat16)

    products[...] = dot(deep_mat[...], grid[...])
    column = lax.broadcasted_iota(jnp.int32, (32, CELLS), 1)
    depth = column % 64

    def tap(b, c):
        return products[pl.ds((b * 3 + c) * 32, 32), :]

    def line(b):
        return (
            tap(b, 1)
            + jnp.where(depth == 0, 0.0, pltpu.roll(tap(b, 0), 1, 1))
            + jnp.where(depth == 63, 0.0, pltpu.roll(tap(b, 2), CELLS - 1, 1))
        )

    pre = line(1)
    pre = pre + jnp.where(column < 64, 0.0, pltpu.roll(line(0), 64, 1))
    pre = pre + jnp.where(column >= CELLS - 64, 0.0, pltpu.roll(line(2), CELLS - 64, 1))
    sigma = 1.0 / (1.0 + jnp.exp(-pre))
    out_ref[...] = (pre * sigma).astype(jnp.bfloat16)
    grad_pre = cot[...].astype(jnp.float32) * sigma * (1.0 + pre * (1.0 - sigma))
    grad_pre = grad_pre.astype(jnp.bfloat16).astype(jnp.float32)
    for b in range(3):
        for c in range(3):
            keep = grad_pre
            if b == 0:
                keep = jnp.where(column < 64, 0.0, keep)
            if b == 2:
                keep = jnp.where(column >= CELLS - 64, 0.0, keep)
            if c == 0:
                keep = jnp.where(depth == 0, 0.0, keep)
            if c == 2:
                keep = jnp.where(depth == 63, 0.0, keep)
            shift = ((b - 1) * 64 + c - 1) % CELLS
            if shift:
                keep = pltpu.roll(keep, shift, 1)
            shifted[pl.ds((b * 3 + c) * 32, 32), :] = keep.astype(jnp.bfloat16)
    local = lax.dot_general(
        shifted[...], grid[...], (((1,), (1,)), ((), ())), preferred_element_type=jnp.float32
    )
    terms[pl.ds(0, 18)] = local[:, 0:128].reshape(18, 16, 128)
    last = jnp.concatenate([local[0:144, 128:192], local[144:288, 128:192]], axis=1)
    terms[pl.ds(18, 9)] = last.reshape(9, 16, 128)

    owner = here < CHUNKS
    for device, to in peers:

        @pl.when(to < CHUNKS)
        def _():
            give(terms.at[to], parts.at[here], 10, 11, at(device, chan))

    @pl.when(owner)
    def _():
        parts[here] = terms[here]
        sized(parts.at[pl.ds(0, PLANE - 1)], sems.at[11]).wait()
        mine[...] = jnp.sum(parts[...], axis=0)
        swap = pltpu.make_async_remote_copy(
            mine, far, sems.at[12], sems.at[13], device_id=at(other, chan), device_id_type=MESH
        )
        swap.start()
        swap.wait_recv()
        sums[here] = (mine[...] + far[...]).astype(jnp.bfloat16)
        for device, _ in peers:
            give(sums.at[here], sums.at[here], 14, 15, at(device, chan))
        swap.wait_send()
        sized(sums.at[pl.ds(0, CHUNKS - 1)], sems.at[15]).wait()
        sized(sums.at[pl.ds(0, PLANE - 1)], sems.at[14]).wait()
        sized(terms.at[pl.ds(0, CHUNKS - 1)], sems.at[10]).wait()

    @pl.when(jnp.logical_not(owner))
    def _():
        sized(sums.at[pl.ds(0, CHUNKS)], sems.at[15]).wait()
        sized(terms, sems.at[10]).wait()

    for block in range(18):
        b, c, half = block // 6, (block // 2) % 3, block % 2
        part = pl.ds(half * 16, 16)
        both = sums[block].astype(jnp.float32)
        grad_ref[0, b, c, part, :] = both[:, 0:64]
        grad_ref[1, b, c, part, :] = both[:, 64:128]
        third = sums[18 + block % 9].astype(jnp.float32)
        grad_ref[2, b, c, part, :] = third[:, 0:64] if block < 9 else third[:, 64:128]

    @pl.when(crossing)
    def _():
        sized(relay, sems.at[19]).wait()
        sized(relay, sems.at[21]).wait()

        @pl.when(opposite > 0)
        def _():
            sized(relay.at[0], sems.at[23]).wait()

        @pl.when(opposite < CHAN - 1)
        def _():
            sized(relay.at[0], sems.at[25]).wait()

    @pl.when(has_side)
    def _():
        sized(pooled.at[0, 0], sems.at[0]).wait()
        sized(pooled.at[0, pl.ds(0, 3)], sems.at[8]).wait()

    sized(pooled.at[0, 0, pl.ds(0, 3)], sems.at[1]).wait()
    sized(pooled.at[0], sems.at[4]).wait()
    sized(pooled.at[0, pl.ds(0, 3)], sems.at[6]).wait()


def on_device(volume, weight_first, weight_deep, cotangent):
    bf16, f32 = jnp.bfloat16, jnp.float32
    deep_out, grad_deep = pl.pallas_call(
        step_kernel,
        out_shape=(
            jax.ShapeDtypeStruct((32, CELLS), bf16),
            jax.ShapeDtypeStruct((3, 3, 3, 32, 64), f32),
        ),
        in_specs=[pl.BlockSpec(memory_space=pl.ANY)]
        + [pl.BlockSpec(memory_space=pltpu.HBM)] * 3,
        out_specs=(
            pl.BlockSpec(memory_space=pltpu.VMEM),
            pl.BlockSpec(memory_space=pltpu.VMEM),
        ),
        scratch_shapes=[
            pltpu.VMEM((4, 4, 32, 128), bf16),
            pltpu.VMEM((2, 32, 128), bf16),
            pltpu.VMEM((3, 3, 3, 32, 64), bf16),
            pltpu.VMEM((3, 3, 3, 32, 64), bf16),
            pltpu.VMEM((32, CELLS), bf16),
            pltpu.VMEM((288, 192), bf16),
            pltpu.VMEM((288, 192), bf16),
            pltpu.VMEM((288, 512), bf16),
            pltpu.VMEM((3, 4, 4, 32, 128), bf16),
            pltpu.VMEM((192, CELLS), bf16),
            pltpu.VMEM((288, CELLS), f32),
            pltpu.VMEM((288, CELLS), bf16),
            pltpu.VMEM((CHUNKS, 16, 128), f32),
            pltpu.VMEM((PLANE, 16, 128), f32),
            pltpu.VMEM((16, 128), f32),
            pltpu.VMEM((16, 128), f32),
            pltpu.VMEM((PLANE, 16, 128), bf16),
            pltpu.SemaphoreType.DMA((4,)),
            pltpu.SemaphoreType.DMA((8,)),
            pltpu.SemaphoreType.DMA((8,)),
            pltpu.SemaphoreType.DMA((31,)),
            pltpu.SemaphoreType.DMA((8,)),
            pltpu.SemaphoreType.REGULAR,
            pltpu.SemaphoreType.REGULAR,
            pltpu.SemaphoreType.REGULAR,
        ],
        compiler_params=pltpu.CompilerParams(
            collective_id=0, has_side_effects=True, vmem_limit_bytes=32 * 2**20
        ),
        name="step",
    )(
        jnp.transpose(volume, (1, 2, 0, 3)),
        jnp.transpose(weight_first, (0, 1, 2, 4, 3)),
        weight_deep,
        cotangent.reshape(32, CELLS),
    )
    return deep_out.reshape(32, 1, CELLS), grad_deep


def solution(mesh):
    return jax.shard_map(
        on_device,
        mesh=mesh,
        in_specs=(
            P(None, "space", "chan", None),
            P(),
            P(None, None, None, "chan", None),
            P("chan", "space", None),
        ),
        out_specs=(P("chan", "space", None), P(None, None, None, "chan", None)),
        check_vma=False,
    )
```

```python
import jax
import jax.numpy as jnp
from jax import lax
from jax.experimental import pallas as pl
from jax.experimental.pallas import tpu as pltpu
from jax.sharding import PartitionSpec as P

MESH = pl.DeviceIdType.MESH
CHUNKS = 27
PLANE = 32
SPACE = 64
CHAN = 16
CELLS = 1024
OFFSETS = sorted(
    [(i, j, k) for i in range(4) for j in range(4) for k in range(2) if (i, j, k) != (0, 0, 0)],
    key=lambda o: (-min(o[0], 4 - o[0]) - min(o[1], 4 - o[1]), o),
)
SIDES = [(dx, dy) for dx in (-1, 0, 1) for dy in (-1, 0, 1) if (dx, dy) != (0, 0)]
SOURCE = {-1: 1, 0: pl.ds(1, 2), 1: 2}
TARGET = {-1: 3, 0: pl.ds(1, 2), 1: 0}


def at(space, chan):
    return {"space": space, "chan": chan}


def sized(ref, sem):
    return pltpu.make_async_copy(ref, ref, sem)


def dot(left, right):
    return jnp.dot(left, right, preferred_element_type=jnp.float32)


def step_kernel(
    vol_in, first_in, deep_in, cot_in, out_ref, grad_ref,
    slab, vol, relay, first, deep, cot, first_mat, deep_mat, windows,
    pooled, grid, products, shifted, terms, parts, mine, far, sums,
    local_sems, halo_send, halo_recv, sems, wide, ready, go, plane,
):
    space = lax.axis_index("space")
    chan = lax.axis_index("chan")
    core = space % 2
    high = (space // 8) % 2
    line, row = space // 16, (space // 2) % 4
    here = line * 8 + row * 2 + core
    other = space + 8 - 16 * high
    rest = chan % 4
    group = chan // 4
    side = space - 1 + 2 * core
    has_side = (side >= 0) & (side < SPACE)
    near, away = 2 * core, 2 - 2 * core

    lines = [(line + step) % 4 for step in range(4)]
    rows = [(row + step) % 4 for step in range(4)]
    cores = [core, 1 - core]
    peers = [
        (lines[i] * 16 + high * 8 + rows[j] * 2 + cores[k], lines[i] * 8 + rows[j] * 2 + cores[k])
        for i, j, k in OFFSETS
    ]
    edge = space % 8
    crossing = has_side & ((edge == 0) | (edge == 7))
    straight = has_side & (edge != 0) & (edge != 7)

    def exists(dx, dy):
        x, y = space + dx, chan + dy
        inside = (x >= 0) & (x < SPACE) & (y >= 0) & (y < CHAN)
        if dx == 0:
            return inside
        return inside & (edge != (7 if dx == 1 else 0))

    def give(src, dst, send, recv, device):
        pltpu.make_async_remote_copy(
            src, dst, sems.at[send], sems.at[recv], device_id=device, device_id_type=MESH
        ).start()

    low = 1 - group // 2
    spots = [group, low * (1 - group) + (1 - low) * (5 - group), 1 + low, 3 * low]
    besides = [group * 4 + (rest + step) % 4 for step in range(4)]
    loads = [
        pltpu.make_async_copy(src, dst, local_sems.at[i])
        for i, (src, dst) in enumerate(
            [
                (first_in, first),
                (deep_in, deep),
                (cot_in, cot),
                (vol_in, vol),
            ]
        )
    ]
    for load in loads:
        load.start()

    barrier = pltpu.get_barrier_semaphore()

    def hello(device):
        pl.semaphore_signal(barrier, inc=1, device_id=device, device_id_type=MESH)

    helper = ((edge == 2) & (space > 2)) | ((edge == 5) & (space < SPACE - 3))
    opposite = (chan + 8) % CHAN
    helper = helper & (high == 0)
    by_relay = crossing & (high == 0)
    direct = crossing & (high == 1)
    hub = opposite + high * (chan - opposite)
    outer = (group == 0) | (group == 3)
    expected = 10 + 3
    for dy in (0, -1, 1):
        meets = crossing & (chan + dy >= 0) & (chan + dy < CHAN)
        met = (helper | direct) & (hub + dy >= 0) & (hub + dy < CHAN)
        expected = expected + jnp.where(met, 1, 0)

        @pl.when(meets)
        def _():
            hello(at(side + high * (4 * core - 2), (chan + dy + 8 * high) % CHAN))

    for dx, dy in SIDES:
        here_too = exists(dx, dy)
        expected = expected + jnp.where(here_too, 1, 0)

        @pl.when(here_too)
        def _():
            hello(at(space + dx, chan + dy))

    for n in range(3):
        close = n < 2 or jnp.logical_not(outer)
        expected = expected + jnp.where(close, 1, 0) + jnp.where(straight & close, 1, 0)

        @pl.when(close)
        def _():
            hello(at(space, spots[n + 1] * 4 + rest))

        @pl.when(straight & close)
        def _():
            hello(at(side, spots[n + 1] * 4 + rest))

    for beside in besides[1:]:
        hello(at(space, beside))

    column = [at(line * 16 + high * 8 + rows[j] * 2 + core, chan) for j in range(1, 4)]
    hello(at(space + 1 - 2 * core, chan))
    for i in range(1, 4):
        for k in range(2):
            hello(at(lines[i] * 16 + high * 8 + row * 2 + cores[k], chan))
    for device in column:
        hello(device)

    @pl.when(space == 0)
    def _():
        slab[0] = jnp.zeros_like(slab[0])
        pooled[0] = jnp.zeros_like(pooled[0])

    @pl.when(space == SPACE - 1)
    def _():
        slab[3] = jnp.zeros_like(slab[3])
        pooled[2] = jnp.zeros_like(pooled[2])

    @pl.when(chan == 0)
    def _():
        slab[:, 0] = jnp.zeros_like(slab[:, 0])

    @pl.when(chan == CHAN - 1)
    def _():
        slab[:, 3] = jnp.zeros_like(slab[:, 3])

    loads[3].wait()
    block = vol[...].astype(jnp.float32)
    for x in range(2):
        for y in range(2):
            slab[1 + x, 1 + y] = block[:, x, y, :].astype(jnp.bfloat16)
    pl.semaphore_wait(barrier, expected)
    pl.semaphore_signal(ready, inc=1, device_id=at(space, opposite), device_id_type=MESH)

    for device in column:
        pl.semaphore_signal(plane, inc=1, device_id=device, device_id_type=MESH)

    @pl.when(helper)
    def _():
        relayed = at(space - 2 + 4 * core, chan)
        pl.semaphore_signal(go, inc=1, device_id=relayed, device_id_type=MESH)

    def rim(n):
        dx, dy = SIDES[n]
        return pltpu.make_async_remote_copy(
            slab.at[SOURCE[dx], SOURCE[dy]],
            slab.at[TARGET[dx], TARGET[dy]],
            halo_send.at[n],
            halo_recv.at[n],
            device_id=at(space + dx, chan + dy),
            device_id_type=MESH,
        )

    for n, (dx, dy) in enumerate(SIDES):

        @pl.when(exists(dx, dy))
        def _():
            rim(n).start()

    ahead, behind = 1 + core, 3 * core
    face = slab.at[ahead, pl.ds(1, 2)]

    def cross(src):
        give(src, slab.at[3 - behind, pl.ds(1, 2)], 21, 22, at(side, hub))

        @pl.when(hub > 0)
        def _():
            give(src.at[0], slab.at[3 - behind, 3], 23, 24, at(side, hub - 1))

        @pl.when(hub < CHAN - 1)
        def _():
            give(src.at[1], slab.at[3 - behind, 0], 25, 26, at(side, hub + 1))

    @pl.when(direct)
    def _():
        cross(face)

    @pl.when(by_relay)
    def _():
        give(face, relay, 19, 20, at(space, opposite))

    for load in loads[:3]:
        load.wait()
    for a in range(3):
        for b in range(3):
            for c in range(3):
                first_mat[pl.ds((a * 3 + b) * 32, 32), pl.ds(c * 64, 64)] = first[a, b, c]
                deep_mat[pl.ds((b * 3 + c) * 32, 32), pl.ds(a * 64, 64)] = deep[a, b, c]

    for n, (dx, dy) in enumerate(SIDES):

        @pl.when(exists(-dx, -dy))
        def _():
            ref = slab.at[TARGET[dx], TARGET[dy]]
            sized(ref, halo_recv.at[n]).wait()

    @pl.when(by_relay)
    def _():
        sized(relay, sems.at[20]).wait()
        pl.semaphore_wait(go, 1)
        cross(relay)

    @pl.when(crossing)
    def _():
        sized(relay, sems.at[22]).wait()

        @pl.when(chan < CHAN - 1)
        def _():
            sized(relay.at[0], sems.at[24]).wait()

        @pl.when(chan > 0)
        def _():
            sized(relay.at[0], sems.at[26]).wait()

    for x in range(2):
        for y in range(2):
            for a in range(3):
                for b in range(3):
                    windows[pl.ds((a * 3 + b) * 32, 32), pl.ds((x * 2 + y) * 128, 128)] = slab[
                        x + a, y + b
                    ]
    taps = lax.dot_general(
        first_mat[...], windows[...], (((0,), (0,)), ((), ())), preferred_element_type=jnp.float32
    )
    z = lax.broadcasted_iota(jnp.int32, (64, 512), 1) % 128
    pre = taps[64:128]
    pre = pre + jnp.where(z == 0, 0.0, pltpu.roll(taps[0:64], 1, 1))
    pre = pre + jnp.where(z == 127, 0.0, pltpu.roll(taps[128:192], 511, 1))
    act = pre / (1.0 + jnp.exp(-pre))
    added = act[:, 0:128] + act[:, 128:256] + act[:, 256:384] + act[:, 384:512]
    mean = ((added + pltpu.roll(added, 127, 1)) * 0.125).astype(jnp.bfloat16)
    lane = lax.broadcasted_iota(jnp.int32, (128, 128), 0)
    cell = lax.broadcasted_iota(jnp.int32, (128, 128), 1)
    left = jnp.where(lane == 2 * cell, 1.0, 0.0).astype(jnp.bfloat16)
    right = jnp.where(lane == 2 * cell - 128, 1.0, 0.0).astype(jnp.bfloat16)
    piece = dot(mean[0:32], left) + dot(mean[32:64], right)
    pooled[1, rest, group] = piece.astype(jnp.bfloat16)

    own = pooled.at[1, rest, group]
    sibling = at(space + 1 - 2 * core, chan)
    flip = jnp.where(crossing, 1, 0)
    turns = [spots[n] + flip * (spots[3 - n] - spots[n]) for n in range(4)]

    def to_mates(plane, index, send, recv):
        for step in (3, 2, 1):
            piece = pooled.at[plane, rest, index]
            give(piece, piece, send, recv, at(space, besides[step]))

    def own_row(n):
        if n:
            sized(own, wide.at[spots[n]]).wait()
        to_mates(1, spots[n], 6, 27 + n)

    def side_row(n):
        @pl.when(has_side)
        def _():
            sized(own, wide.at[4 + turns[n]]).wait()
            to_mates(near, turns[n], 8, 9)

    def to_sibling(n):
        sized(pooled.at[0, 0, pl.ds(0, 3)], sems.at[27 + n]).wait()
        give(pooled.at[1, :, spots[n]], pooled.at[near, :, spots[n]], 4, 5, sibling)

    pl.semaphore_wait(ready, 1)
    pl.semaphore_wait(plane, 3)
    for n in (3, 2, 1):
        pltpu.make_async_remote_copy(
            own, own, sems.at[1], wide.at[group],
            device_id=at(space, spots[n] * 4 + rest), device_id_type=MESH,
        ).start()

    def to_side(n):
        pltpu.make_async_remote_copy(
            own, pooled.at[away, rest, group], sems.at[0], wide.at[4 + group],
            device_id=at(side, spots[n] * 4 + rest), device_id_type=MESH,
        ).start()

    later = by_relay & outer

    @pl.when(has_side & jnp.logical_not(later))
    def _():
        to_side(3)

    @pl.when(has_side)
    def _():
        for n in (2, 1, 0):
            to_side(n)

    own_row(0)
    own_row(1)
    to_sibling(0)
    own_row(2)

    @pl.when(later)
    def _():
        to_side(3)

    side_row(0)
    to_sibling(1)
    side_row(1)
    own_row(3)
    to_sibling(2)
    side_row(2)
    side_row(3)
    to_sibling(3)

    lanes = lax.broadcasted_iota(jnp.int32, (32, 128), 1)

    def lay_out(a):
        for pair in range(8):
            rows = [
                pooled[a, row % 4, row // 4].astype(jnp.float32) for row in (2 * pair, 2 * pair + 1)
            ]
            low = jnp.where(lanes < 64, rows[0], pltpu.roll(rows[1], 64, 1))
            top = jnp.where(lanes < 64, pltpu.roll(rows[0], 64, 1), rows[1])
            grid[pl.ds(a * 64, 32), pl.ds(pair * 128, 128)] = low.astype(jnp.bfloat16)
            grid[pl.ds(a * 64 + 32, 32), pl.ds(pair * 128, 128)] = top.astype(jnp.bfloat16)

    lay_out(1)

    @pl.when(has_side)
    def _():
        sized(pooled.at[0, pl.ds(0, 3)], sems.at[9]).wait()

    sized(pooled.at[0], sems.at[5]).wait()

    lay_out(0)
    lay_out(2)

    products[...] = dot(deep_mat[...], grid[...])
    column = lax.broadcasted_iota(jnp.int32, (32, CELLS), 1)
    depth = column % 64

    def tap(b, c):
        return products[pl.ds((b * 3 + c) * 32, 32), :]

    def line(b):
        return (
            tap(b, 1)
            + jnp.where(depth == 0, 0.0, pltpu.roll(tap(b, 0), 1, 1))
            + jnp.where(depth == 63, 0.0, pltpu.roll(tap(b, 2), CELLS - 1, 1))
        )

    pre = line(1)
    pre = pre + jnp.where(column < 64, 0.0, pltpu.roll(line(0), 64, 1))
    pre = pre + jnp.where(column >= CELLS - 64, 0.0, pltpu.roll(line(2), CELLS - 64, 1))
    sigma = 1.0 / (1.0 + jnp.exp(-pre))
    grad_pre = cot[...].astype(jnp.float32) * sigma * (1.0 + pre * (1.0 - sigma))
    grad_pre = grad_pre.astype(jnp.bfloat16).astype(jnp.float32)
    for b in range(3):
        for c in range(3):
            keep = grad_pre
            if b == 0:
                keep = jnp.where(column < 64, 0.0, keep)
            if b == 2:
                keep = jnp.where(column >= CELLS - 64, 0.0, keep)
            if c == 0:
                keep = jnp.where(depth == 0, 0.0, keep)
            if c == 2:
                keep = jnp.where(depth == 63, 0.0, keep)
            shift = ((b - 1) * 64 + c - 1) % CELLS
            if shift:
                keep = pltpu.roll(keep, shift, 1)
            shifted[pl.ds((b * 3 + c) * 32, 32), :] = keep.astype(jnp.bfloat16)
    local = lax.dot_general(
        shifted[...], grid[...], (((1,), (1,)), ((), ())), preferred_element_type=jnp.float32
    )
    terms[pl.ds(0, 18)] = local[:, 0:128].reshape(18, 16, 128)
    last = jnp.concatenate([local[0:144, 128:192], local[144:288, 128:192]], axis=1)
    terms[pl.ds(18, 9)] = last.reshape(9, 16, 128)

    owner = here < CHUNKS
    for device, to in peers:

        @pl.when(to < CHUNKS)
        def _():
            give(terms.at[to], parts.at[here], 10, 11, at(device, chan))

    out_ref[...] = (pre * sigma).astype(jnp.bfloat16)

    @pl.when(owner)
    def _():
        parts[here] = terms[here]
        sized(parts.at[pl.ds(0, PLANE - 1)], sems.at[11]).wait()
        mine[...] = jnp.sum(parts[...], axis=0)
        swap = pltpu.make_async_remote_copy(
            mine, far, sems.at[12], sems.at[13], device_id=at(other, chan), device_id_type=MESH
        )
        swap.start()
        swap.wait_recv()
        sums[here] = (mine[...] + far[...]).astype(jnp.bfloat16)
        for device, _ in peers:
            give(sums.at[here], sums.at[here], 14, 15, at(device, chan))
        swap.wait_send()
        sized(sums.at[pl.ds(0, CHUNKS - 1)], sems.at[15]).wait()
        sized(sums.at[pl.ds(0, PLANE - 1)], sems.at[14]).wait()
        sized(terms.at[pl.ds(0, CHUNKS - 1)], sems.at[10]).wait()

    @pl.when(jnp.logical_not(owner))
    def _():
        sized(sums.at[pl.ds(0, CHUNKS)], sems.at[15]).wait()
        sized(terms, sems.at[10]).wait()

    for block in range(18):
        b, c, half = block // 6, (block // 2) % 3, block % 2
        part = pl.ds(half * 16, 16)
        both = sums[block].astype(jnp.float32)
        grad_ref[0, b, c, part, :] = both[:, 0:64]
        grad_ref[1, b, c, part, :] = both[:, 64:128]
        third = sums[18 + block % 9].astype(jnp.float32)
        grad_ref[2, b, c, part, :] = third[:, 0:64] if block < 9 else third[:, 64:128]

    for n, (dx, dy) in enumerate(SIDES):

        @pl.when(exists(dx, dy))
        def _():
            ref = slab.at[SOURCE[dx], SOURCE[dy]]
            sized(ref, halo_send.at[n]).wait()

    @pl.when(by_relay)
    def _():
        sized(relay, sems.at[19]).wait()

    @pl.when(crossing)
    def _():
        sized(relay, sems.at[21]).wait()

        @pl.when(hub > 0)
        def _():
            sized(relay.at[0], sems.at[23]).wait()

        @pl.when(hub < CHAN - 1)
        def _():
            sized(relay.at[0], sems.at[25]).wait()

    @pl.when(has_side)
    def _():
        sized(pooled.at[0, 0], sems.at[0]).wait()
        sized(pooled.at[0, pl.ds(0, 3)], sems.at[8]).wait()

    sized(pooled.at[0, 0, pl.ds(0, 3)], sems.at[1]).wait()
    sized(pooled.at[0], sems.at[4]).wait()
    sized(pooled.at[0, pl.ds(0, 3)], sems.at[6]).wait()


def on_device(volume, weight_first, weight_deep, cotangent):
    bf16, f32 = jnp.bfloat16, jnp.float32
    deep_out, grad_deep = pl.pallas_call(
        step_kernel,
        out_shape=(
            jax.ShapeDtypeStruct((32, CELLS), bf16),
            jax.ShapeDtypeStruct((3, 3, 3, 32, 64), f32),
        ),
        in_specs=[pl.BlockSpec(memory_space=pltpu.HBM)]
        + [pl.BlockSpec(memory_space=pltpu.HBM)] * 3,
        out_specs=(
            pl.BlockSpec(memory_space=pltpu.VMEM),
            pl.BlockSpec(memory_space=pltpu.VMEM),
        ),
        scratch_shapes=[
            pltpu.VMEM((4, 4, 32, 128), bf16),
            pltpu.VMEM((32, 2, 2, 128), bf16),
            pltpu.VMEM((2, 32, 128), bf16),
            pltpu.VMEM((3, 3, 3, 32, 64), bf16),
            pltpu.VMEM((3, 3, 3, 32, 64), bf16),
            pltpu.VMEM((32, CELLS), bf16),
            pltpu.VMEM((288, 192), bf16),
            pltpu.VMEM((288, 192), bf16),
            pltpu.VMEM((288, 512), bf16),
            pltpu.VMEM((3, 4, 4, 32, 128), bf16),
            pltpu.VMEM((192, CELLS), bf16),
            pltpu.VMEM((288, CELLS), f32),
            pltpu.VMEM((288, CELLS), bf16),
            pltpu.VMEM((CHUNKS, 16, 128), f32),
            pltpu.VMEM((PLANE, 16, 128), f32),
            pltpu.VMEM((16, 128), f32),
            pltpu.VMEM((16, 128), f32),
            pltpu.VMEM((PLANE, 16, 128), bf16),
            pltpu.SemaphoreType.DMA((4,)),
            pltpu.SemaphoreType.DMA((8,)),
            pltpu.SemaphoreType.DMA((8,)),
            pltpu.SemaphoreType.DMA((31,)),
            pltpu.SemaphoreType.DMA((8,)),
            pltpu.SemaphoreType.REGULAR,
            pltpu.SemaphoreType.REGULAR,
            pltpu.SemaphoreType.REGULAR,
        ],
        compiler_params=pltpu.CompilerParams(
            collective_id=0, has_side_effects=True, vmem_limit_bytes=55500 * 1024
        ),
        name="step",
    )(
        volume,
        jnp.transpose(weight_first, (0, 1, 2, 4, 3)),
        weight_deep,
        cotangent.reshape(32, CELLS),
    )
    return deep_out.reshape(32, 1, CELLS), grad_deep


def solution(mesh):
    return jax.shard_map(
        on_device,
        mesh=mesh,
        in_specs=(
            P(None, "space", "chan", None),
            P(),
            P(None, None, None, "chan", None),
            P("chan", "space", None),
        ),
        out_specs=(P("chan", "space", None), P(None, None, None, "chan", None)),
        check_vma=False,
    )
```

```python
import jax
import jax.numpy as jnp
from jax import lax
from jax.experimental import pallas as pl
from jax.experimental.pallas import tpu as pltpu
from jax.sharding import PartitionSpec as P

MESH = pl.DeviceIdType.MESH
CHUNKS = 27
PLANE = 32
SPACE = 64
CHAN = 16
CELLS = 1024
OFFSETS = sorted(
    [(i, j, k) for i in range(4) for j in range(4) for k in range(2) if (i, j, k) != (0, 0, 0)],
    key=lambda o: (-min(o[0], 4 - o[0]) - min(o[1], 4 - o[1]), o),
)
SIDES = [(dx, dy) for dx in (-1, 0, 1) for dy in (-1, 0, 1) if (dx, dy) != (0, 0)]
SOURCE = {-1: 1, 0: pl.ds(1, 2), 1: 2}
TARGET = {-1: 3, 0: pl.ds(1, 2), 1: 0}


def at(space, chan):
    return {"space": space, "chan": chan}


def sized(ref, sem):
    return pltpu.make_async_copy(ref, ref, sem)


def dot(left, right):
    return jnp.dot(left, right, preferred_element_type=jnp.float32)


def step_kernel(
    vol_in, first_in, deep_in, cot_in, out_ref, grad_ref,
    slab, vol, relay, first, deep, cot, first_mat, deep_mat, windows,
    pooled, grid, products, shifted, terms, parts, mine, far, sums,
    local_sems, halo_send, halo_recv, sems, wide, ready, go, plane,
):
    space = lax.axis_index("space")
    chan = lax.axis_index("chan")
    core = space % 2
    high = (space // 8) % 2
    line, row = space // 16, (space // 2) % 4
    here = line * 8 + row * 2 + core
    other = space + 8 - 16 * high
    rest = chan % 4
    group = chan // 4
    side = space - 1 + 2 * core
    has_side = (side >= 0) & (side < SPACE)
    near, away = 2 * core, 2 - 2 * core

    lines = [(line + step) % 4 for step in range(4)]
    rows = [(row + step) % 4 for step in range(4)]
    cores = [core, 1 - core]
    peers = [
        (lines[i] * 16 + high * 8 + rows[j] * 2 + cores[k], lines[i] * 8 + rows[j] * 2 + cores[k])
        for i, j, k in OFFSETS
    ]
    edge = space % 8
    crossing = has_side & ((edge == 0) | (edge == 7))
    straight = has_side & (edge != 0) & (edge != 7)

    def exists(dx, dy):
        x, y = space + dx, chan + dy
        inside = (x >= 0) & (x < SPACE) & (y >= 0) & (y < CHAN)
        if dx == 0:
            return inside
        return inside & (edge != (7 if dx == 1 else 0))

    def give(src, dst, send, recv, device):
        pltpu.make_async_remote_copy(
            src, dst, sems.at[send], sems.at[recv], device_id=device, device_id_type=MESH
        ).start()

    low = 1 - group // 2
    spots = [group, low * (1 - group) + (1 - low) * (5 - group), 1 + low, 3 * low]
    besides = [group * 4 + (rest + step) % 4 for step in range(4)]
    loads = [
        pltpu.make_async_copy(src, dst, local_sems.at[i])
        for i, (src, dst) in enumerate(
            [
                (vol_in, vol),
                (first_in, first),
                (deep_in, deep),
                (cot_in, cot),
            ]
        )
    ]
    for load in loads:
        load.start()

    barrier = pltpu.get_barrier_semaphore()

    def hello(device):
        pl.semaphore_signal(barrier, inc=1, device_id=device, device_id_type=MESH)

    helper = ((edge == 2) & (space > 2)) | ((edge == 5) & (space < SPACE - 3))
    opposite = (chan + 8) % CHAN
    outer = (group == 0) | (group == 3)
    expected = 10 + 3
    for dy in (0, -1, 1):
        meets = crossing & (chan + dy >= 0) & (chan + dy < CHAN)
        met = helper & (opposite + dy >= 0) & (opposite + dy < CHAN)
        expected = expected + jnp.where(met, 1, 0)

        @pl.when(meets)
        def _():
            hello(at(side - 2 + 4 * core, (chan + dy + 8) % CHAN))

    for dx, dy in SIDES:
        here_too = exists(dx, dy)
        expected = expected + jnp.where(here_too, 1, 0)

        @pl.when(here_too)
        def _():
            hello(at(space + dx, chan + dy))

    for n in range(3):
        close = n < 2 or jnp.logical_not(outer)
        expected = expected + jnp.where(close, 1, 0) + jnp.where(straight & close, 1, 0)

        @pl.when(close)
        def _():
            hello(at(space, spots[n + 1] * 4 + rest))

        @pl.when(straight & close)
        def _():
            hello(at(side, spots[n + 1] * 4 + rest))

    for beside in besides[1:]:
        hello(at(space, beside))

    column = [at(line * 16 + high * 8 + rows[j] * 2 + core, chan) for j in range(1, 4)]
    hello(at(space + 1 - 2 * core, chan))
    for i in range(1, 4):
        for k in range(2):
            hello(at(lines[i] * 16 + high * 8 + row * 2 + cores[k], chan))
    for device in column:
        hello(device)

    @pl.when(space == 0)
    def _():
        slab[0] = jnp.zeros_like(slab[0])
        pooled[0] = jnp.zeros_like(pooled[0])

    @pl.when(space == SPACE - 1)
    def _():
        slab[3] = jnp.zeros_like(slab[3])
        pooled[2] = jnp.zeros_like(pooled[2])

    @pl.when(chan == 0)
    def _():
        slab[:, 0] = jnp.zeros_like(slab[:, 0])

    @pl.when(chan == CHAN - 1)
    def _():
        slab[:, 3] = jnp.zeros_like(slab[:, 3])

    loads[0].wait()
    block = vol[...].astype(jnp.float32)
    for x in range(2):
        for y in range(2):
            slab[1 + x, 1 + y] = block[:, x, y, :].astype(jnp.bfloat16)
    pl.semaphore_wait(barrier, expected)
    pl.semaphore_signal(ready, inc=1, device_id=at(space, opposite), device_id_type=MESH)

    for device in column:
        pl.semaphore_signal(plane, inc=1, device_id=device, device_id_type=MESH)

    @pl.when(helper)
    def _():
        relayed = at(space - 2 + 4 * core, chan)
        pl.semaphore_signal(go, inc=1, device_id=relayed, device_id_type=MESH)

    def rim(n):
        dx, dy = SIDES[n]
        return pltpu.make_async_remote_copy(
            slab.at[SOURCE[dx], SOURCE[dy]],
            slab.at[TARGET[dx], TARGET[dy]],
            halo_send.at[n],
            halo_recv.at[n],
            device_id=at(space + dx, chan + dy),
            device_id_type=MESH,
        )

    for n, (dx, dy) in enumerate(SIDES):

        @pl.when(exists(dx, dy))
        def _():
            rim(n).start()

    ahead, behind = 1 + core, 3 * core
    face = slab.at[ahead, pl.ds(1, 2)]

    @pl.when(crossing)
    def _():
        give(face, relay, 19, 20, at(space, opposite))

    for load in loads[1:]:
        load.wait()
    for a in range(3):
        for b in range(3):
            for c in range(3):
                first_mat[pl.ds((a * 3 + b) * 32, 32), pl.ds(c * 64, 64)] = first[a, b, c]
                deep_mat[pl.ds((b * 3 + c) * 32, 32), pl.ds(a * 64, 64)] = deep[a, b, c]

    for n, (dx, dy) in enumerate(SIDES):

        @pl.when(exists(-dx, -dy))
        def _():
            ref = slab.at[TARGET[dx], TARGET[dy]]
            sized(ref, halo_recv.at[n]).wait()

    @pl.when(crossing)
    def _():
        sized(relay, sems.at[20]).wait()
        pl.semaphore_wait(go, 1)
        give(relay, slab.at[3 - behind, pl.ds(1, 2)], 21, 22, at(side, opposite))

        @pl.when(opposite > 0)
        def _():
            give(relay.at[0], slab.at[3 - behind, 3], 23, 24, at(side, opposite - 1))

        @pl.when(opposite < CHAN - 1)
        def _():
            give(relay.at[1], slab.at[3 - behind, 0], 25, 26, at(side, opposite + 1))

        sized(relay, sems.at[22]).wait()

        @pl.when(chan < CHAN - 1)
        def _():
            sized(relay.at[0], sems.at[24]).wait()

        @pl.when(chan > 0)
        def _():
            sized(relay.at[0], sems.at[26]).wait()

    for x in range(2):
        for y in range(2):
            for a in range(3):
                for b in range(3):
                    windows[pl.ds((a * 3 + b) * 32, 32), pl.ds((x * 2 + y) * 128, 128)] = slab[
                        x + a, y + b
                    ]
    taps = lax.dot_general(
        first_mat[...], windows[...], (((0,), (0,)), ((), ())), preferred_element_type=jnp.float32
    )
    z = lax.broadcasted_iota(jnp.int32, (64, 512), 1) % 128
    pre = taps[64:128]
    pre = pre + jnp.where(z == 0, 0.0, pltpu.roll(taps[0:64], 1, 1))
    pre = pre + jnp.where(z == 127, 0.0, pltpu.roll(taps[128:192], 511, 1))
    act = pre / (1.0 + jnp.exp(-pre))
    added = act[:, 0:128] + act[:, 128:256] + act[:, 256:384] + act[:, 384:512]
    mean = ((added + pltpu.roll(added, 127, 1)) * 0.125).astype(jnp.bfloat16)
    lane = lax.broadcasted_iota(jnp.int32, (128, 128), 0)
    cell = lax.broadcasted_iota(jnp.int32, (128, 128), 1)
    left = jnp.where(lane == 2 * cell, 1.0, 0.0).astype(jnp.bfloat16)
    right = jnp.where(lane == 2 * cell - 128, 1.0, 0.0).astype(jnp.bfloat16)
    piece = dot(mean[0:32], left) + dot(mean[32:64], right)
    pooled[1, rest, group] = piece.astype(jnp.bfloat16)

    own = pooled.at[1, rest, group]
    sibling = at(space + 1 - 2 * core, chan)
    flip = jnp.where(crossing, 1, 0)
    turns = [spots[n] + flip * (spots[3 - n] - spots[n]) for n in range(4)]

    def to_mates(plane, index, send, recv):
        for step in (3, 2, 1):
            piece = pooled.at[plane, rest, index]
            give(piece, piece, send, recv, at(space, besides[step]))

    def own_row(n):
        if n:
            sized(own, wide.at[spots[n]]).wait()
        to_mates(1, spots[n], 6, 27 + n)

    def side_row(n):
        @pl.when(has_side)
        def _():
            sized(own, wide.at[4 + turns[n]]).wait()
            to_mates(near, turns[n], 8, 9)

    def to_sibling(n):
        sized(pooled.at[0, 0, pl.ds(0, 3)], sems.at[27 + n]).wait()
        give(pooled.at[1, :, spots[n]], pooled.at[near, :, spots[n]], 4, 5, sibling)

    pl.semaphore_wait(ready, 1)
    pl.semaphore_wait(plane, 3)
    for n in (3, 2, 1):
        pltpu.make_async_remote_copy(
            own, own, sems.at[1], wide.at[group],
            device_id=at(space, spots[n] * 4 + rest), device_id_type=MESH,
        ).start()

    @pl.when(has_side)
    def _():
        for n in (3, 2, 1, 0):
            pltpu.make_async_remote_copy(
                own, pooled.at[away, rest, group], sems.at[0], wide.at[4 + group],
                device_id=at(side, spots[n] * 4 + rest), device_id_type=MESH,
            ).start()

    own_row(0)
    for n in range(1, 4):
        side_row(n - 1)
        own_row(n)
        to_sibling(n - 1)
    side_row(3)
    to_sibling(3)

    lanes = lax.broadcasted_iota(jnp.int32, (32, 128), 1)

    def lay_out(a):
        for pair in range(8):
            rows = [
                pooled[a, row % 4, row // 4].astype(jnp.float32) for row in (2 * pair, 2 * pair + 1)
            ]
            low = jnp.where(lanes < 64, rows[0], pltpu.roll(rows[1], 64, 1))
            top = jnp.where(lanes < 64, pltpu.roll(rows[0], 64, 1), rows[1])
            grid[pl.ds(a * 64, 32), pl.ds(pair * 128, 128)] = low.astype(jnp.bfloat16)
            grid[pl.ds(a * 64 + 32, 32), pl.ds(pair * 128, 128)] = top.astype(jnp.bfloat16)

    lay_out(1)

    @pl.when(has_side)
    def _():
        sized(pooled.at[0, pl.ds(0, 3)], sems.at[9]).wait()

    sized(pooled.at[0], sems.at[5]).wait()

    lay_out(0)
    lay_out(2)

    products[...] = dot(deep_mat[...], grid[...])
    column = lax.broadcasted_iota(jnp.int32, (32, CELLS), 1)
    depth = column % 64

    def tap(b, c):
        return products[pl.ds((b * 3 + c) * 32, 32), :]

    def line(b):
        return (
            tap(b, 1)
            + jnp.where(depth == 0, 0.0, pltpu.roll(tap(b, 0), 1, 1))
            + jnp.where(depth == 63, 0.0, pltpu.roll(tap(b, 2), CELLS - 1, 1))
        )

    pre = line(1)
    pre = pre + jnp.where(column < 64, 0.0, pltpu.roll(line(0), 64, 1))
    pre = pre + jnp.where(column >= CELLS - 64, 0.0, pltpu.roll(line(2), CELLS - 64, 1))
    sigma = 1.0 / (1.0 + jnp.exp(-pre))
    grad_pre = cot[...].astype(jnp.float32) * sigma * (1.0 + pre * (1.0 - sigma))
    grad_pre = grad_pre.astype(jnp.bfloat16).astype(jnp.float32)
    for b in range(3):
        for c in range(3):
            keep = grad_pre
            if b == 0:
                keep = jnp.where(column < 64, 0.0, keep)
            if b == 2:
                keep = jnp.where(column >= CELLS - 64, 0.0, keep)
            if c == 0:
                keep = jnp.where(depth == 0, 0.0, keep)
            if c == 2:
                keep = jnp.where(depth == 63, 0.0, keep)
            shift = ((b - 1) * 64 + c - 1) % CELLS
            if shift:
                keep = pltpu.roll(keep, shift, 1)
            shifted[pl.ds((b * 3 + c) * 32, 32), :] = keep.astype(jnp.bfloat16)
    local = lax.dot_general(
        shifted[...], grid[...], (((1,), (1,)), ((), ())), preferred_element_type=jnp.float32
    )
    terms[pl.ds(0, 18)] = local[:, 0:128].reshape(18, 16, 128)
    last = jnp.concatenate([local[0:144, 128:192], local[144:288, 128:192]], axis=1)
    terms[pl.ds(18, 9)] = last.reshape(9, 16, 128)

    owner = here < CHUNKS
    for device, to in peers:

        @pl.when(to < CHUNKS)
        def _():
            give(terms.at[to], parts.at[here], 10, 11, at(device, chan))

    out_ref[...] = (pre * sigma).astype(jnp.bfloat16)

    @pl.when(owner)
    def _():
        parts[here] = terms[here]
        sized(parts.at[pl.ds(0, PLANE - 1)], sems.at[11]).wait()
        mine[...] = jnp.sum(parts[...], axis=0)
        swap = pltpu.make_async_remote_copy(
            mine, far, sems.at[12], sems.at[13], device_id=at(other, chan), device_id_type=MESH
        )
        swap.start()
        swap.wait_recv()
        sums[here] = (mine[...] + far[...]).astype(jnp.bfloat16)
        for device, _ in peers:
            give(sums.at[here], sums.at[here], 14, 15, at(device, chan))
        swap.wait_send()
        sized(sums.at[pl.ds(0, CHUNKS - 1)], sems.at[15]).wait()
        sized(sums.at[pl.ds(0, PLANE - 1)], sems.at[14]).wait()
        sized(terms.at[pl.ds(0, CHUNKS - 1)], sems.at[10]).wait()

    @pl.when(jnp.logical_not(owner))
    def _():
        sized(sums.at[pl.ds(0, CHUNKS)], sems.at[15]).wait()
        sized(terms, sems.at[10]).wait()

    for block in range(18):
        b, c, half = block // 6, (block // 2) % 3, block % 2
        part = pl.ds(half * 16, 16)
        both = sums[block].astype(jnp.float32)
        grad_ref[0, b, c, part, :] = both[:, 0:64]
        grad_ref[1, b, c, part, :] = both[:, 64:128]
        third = sums[18 + block % 9].astype(jnp.float32)
        grad_ref[2, b, c, part, :] = third[:, 0:64] if block < 9 else third[:, 64:128]

    for n, (dx, dy) in enumerate(SIDES):

        @pl.when(exists(dx, dy))
        def _():
            ref = slab.at[SOURCE[dx], SOURCE[dy]]
            sized(ref, halo_send.at[n]).wait()

    @pl.when(crossing)
    def _():
        sized(relay, sems.at[19]).wait()
        sized(relay, sems.at[21]).wait()

        @pl.when(opposite > 0)
        def _():
            sized(relay.at[0], sems.at[23]).wait()

        @pl.when(opposite < CHAN - 1)
        def _():
            sized(relay.at[0], sems.at[25]).wait()

    @pl.when(has_side)
    def _():
        sized(pooled.at[0, 0], sems.at[0]).wait()
        sized(pooled.at[0, pl.ds(0, 3)], sems.at[8]).wait()

    sized(pooled.at[0, 0, pl.ds(0, 3)], sems.at[1]).wait()
    sized(pooled.at[0], sems.at[4]).wait()
    sized(pooled.at[0, pl.ds(0, 3)], sems.at[6]).wait()


def on_device(volume, weight_first, weight_deep, cotangent):
    bf16, f32 = jnp.bfloat16, jnp.float32
    deep_out, grad_deep = pl.pallas_call(
        step_kernel,
        out_shape=(
            jax.ShapeDtypeStruct((32, CELLS), bf16),
            jax.ShapeDtypeStruct((3, 3, 3, 32, 64), f32),
        ),
        in_specs=[pl.BlockSpec(memory_space=pltpu.HBM)]
        + [pl.BlockSpec(memory_space=pltpu.HBM)] * 3,
        out_specs=(
            pl.BlockSpec(memory_space=pltpu.VMEM),
            pl.BlockSpec(memory_space=pltpu.VMEM),
        ),
        scratch_shapes=[
            pltpu.VMEM((4, 4, 32, 128), bf16),
            pltpu.VMEM((32, 2, 2, 128), bf16),
            pltpu.VMEM((2, 32, 128), bf16),
            pltpu.VMEM((3, 3, 3, 32, 64), bf16),
            pltpu.VMEM((3, 3, 3, 32, 64), bf16),
            pltpu.VMEM((32, CELLS), bf16),
            pltpu.VMEM((288, 192), bf16),
            pltpu.VMEM((288, 192), bf16),
            pltpu.VMEM((288, 512), bf16),
            pltpu.VMEM((3, 4, 4, 32, 128), bf16),
            pltpu.VMEM((192, CELLS), bf16),
            pltpu.VMEM((288, CELLS), f32),
            pltpu.VMEM((288, CELLS), bf16),
            pltpu.VMEM((CHUNKS, 16, 128), f32),
            pltpu.VMEM((PLANE, 16, 128), f32),
            pltpu.VMEM((16, 128), f32),
            pltpu.VMEM((16, 128), f32),
            pltpu.VMEM((PLANE, 16, 128), bf16),
            pltpu.SemaphoreType.DMA((4,)),
            pltpu.SemaphoreType.DMA((8,)),
            pltpu.SemaphoreType.DMA((8,)),
            pltpu.SemaphoreType.DMA((31,)),
            pltpu.SemaphoreType.DMA((8,)),
            pltpu.SemaphoreType.REGULAR,
            pltpu.SemaphoreType.REGULAR,
            pltpu.SemaphoreType.REGULAR,
        ],
        compiler_params=pltpu.CompilerParams(
            collective_id=0, has_side_effects=True, vmem_limit_bytes=55500 * 1024
        ),
        name="step",
    )(
        volume,
        jnp.transpose(weight_first, (0, 1, 2, 4, 3)),
        weight_deep,
        cotangent.reshape(32, CELLS),
    )
    return deep_out.reshape(32, 1, CELLS), grad_deep


def solution(mesh):
    return jax.shard_map(
        on_device,
        mesh=mesh,
        in_specs=(
            P(None, "space", "chan", None),
            P(),
            P(None, None, None, "chan", None),
            P("chan", "space", None),
        ),
        out_specs=(P("chan", "space", None), P(None, None, None, "chan", None)),
        check_vma=False,
    )
```
